128 devices in a mesh: outer: 8 (over y, core), inner: 16 (over z, x).
Axes of the slice: x: 4, y: 4, z: 4, core: 2. Of those that a mesh axis runs over, the one named last changes fastest.
Arguments:
- queries: bfloat16 [16384, 2048], P(('outer', 'inner')), may hold values from -6 to 6
- key_vectors: bfloat16 [16384, 2048], P(('outer', 'inner')), may hold values from -6 to 6
- value_vectors: bfloat16 [16384, 2048], P(('outer', 'inner')), may hold values from -6 to 6
- segment_ids: int32 [16384], P(('outer', 'inner')), may hold values from 0 to 15, never falling along the last dimension, each value on 1 to 4096 neighbouring positions
- ridge_weight: float32 [16], replicated, may hold values from 2 to 32
Outputs:
- readout: float32 [16384, 2048], P(('outer', 'inner'))
The draws below stay inside these ranges and needn't reach their ends.
Inputs may be any that keep to these rules, and one draw needn't show every extreme that they name: `segment_ids`: segment ids never fall along the sequence; each document has 1 to 4096 tokens and one has exactly 4096.
All inputs are finite; a program needn't handle non-finite values.
Results may differ from the reference program's by a relative error of at most 0.0003.
Values sent between devices are 32-bit elements; how exact they have to be, the bound alone decides.
A program may use at most 128 MiB of HBM per device.

```python
import math
import jax
import jax.numpy as jnp
import numpy as np
from jax import lax

H = 16
E = 128
CG_ITERS = 3
DOCS = 16
TOKENS = 16384
DOC_MOST = 4096


def levels(own_key, shape, cuts, low, top_value):
    factor_of = 1.0
    for dim, blocks in cuts:
        steps = jax.random.uniform(jax.random.fold_in(jax.random.fold_in(own_key, 6), dim), (blocks,), jnp.float32, low / len(cuts), top_value / len(cuts))
        factor_of = factor_of * jnp.repeat(jnp.exp(steps), shape[dim] // blocks).reshape((-1,) + (1,) * (len(shape) - 1 - dim))
    return factor_of


def split_up(amount, total, most, skew):
    portions = [(1 << 20) // math.isqrt(rank ** skew) + 1 for rank in range(2, amount + 1)]
    surplus, given = total - most - (amount - 1), [1] * (amount - 1)
    while surplus > 0:
        candidates = [i for i in range(amount - 1) if given[i] < most]
        mass, left = sum([portions[i] for i in candidates]), surplus
        for i in candidates:
            addition = min(most - given[i], max(1, left * portions[i] // mass), surplus)
            given[i] = given[i] + addition
            surplus = surplus - addition
    return np.array([most] + given)


def uneven(rng, number_of, total, limit, skew):
    if number_of == 2:
        one = jax.random.randint(rng, (), max(1, total - limit), min(limit, total - 1) + 1)
        return jnp.stack([one, total - one])
    lengths = jnp.asarray(split_up(number_of, total, limit, skew), jnp.int32)
    twos = (number_of - 1) // 2
    source_of, sink = lengths[1:1 + 2 * twos:2], lengths[2:2 + 2 * twos:2]
    room = jnp.minimum(source_of - 1, limit - sink)
    shifted = jax.random.randint(jax.random.fold_in(rng, 1), (twos,), 0, 1 << 20) % (room + 1)
    lengths = lengths.at[1:1 + 2 * twos:2].set(source_of - shifted).at[2:2 + 2 * twos:2].set(sink + shifted)
    return lengths[jax.random.permutation(jax.random.fold_in(rng, 2), number_of)]


def noise(key, dims, scale, most, split=(), dtype=jnp.bfloat16):
    entries = scale * jax.random.normal(key, dims, jnp.float32)
    if split:
        entries = entries * levels(key, dims, split, -0.22, 0.18)
    return jnp.clip(entries, -most, most).astype(dtype)


def setup_inputs(seed: int = 0) -> dict:
    keys = jax.random.split(jax.random.key(seed), 6)
    queries = noise(keys[0], (TOKENS, H * E), 1.0, 6.0, ((0, 128),))
    key_vectors = noise(keys[1], (TOKENS, H * E), 1.0, 6.0, ((0, 128),))
    value_vectors = noise(keys[2], (TOKENS, H * E), 1.0, 6.0, ((0, 128),))
    segment_ids = jnp.searchsorted(jnp.cumsum(uneven(keys[3], DOCS, TOKENS, DOC_MOST, 1)), jnp.arange(TOKENS), side="right").astype(jnp.int32)
    ridge_weight = jnp.clip(jnp.exp(jax.random.uniform(keys[4], (H,), jnp.float32, math.log(2.0), math.log(32.0))), 2.0, 32.0)
    return dict(queries=queries, key_vectors=key_vectors, value_vectors=value_vectors, segment_ids=segment_ids, ridge_weight=ridge_weight)


highest = lax.Precision.HIGHEST
block_rows = 128

def normed(values_in):
    widened = values_in.astype(jnp.float32)
    return widened * lax.rsqrt(lax.optimization_barrier(jnp.sum(widened * widened, -1, keepdims=True)) + 1e-06)

def combine(earlier, latter):
    early_last, early_gram, early_cross = earlier
    late_last, late_gram, late_cross = latter
    keep_mask = jnp.logical_or(early_last == late_last, late_last < 0).astype(jnp.float32)
    return (jnp.where(late_last < 0, early_last, late_last), late_gram + keep_mask * early_gram, late_cross + keep_mask * early_cross)

def summarize(key_rows, value_rows, segment):
    last_value = segment[-1]
    weight = (segment == last_value).astype(jnp.float32)[None, :, None]
    gram = jnp.einsum('hbe,hbf->hef', key_rows * weight, key_rows, precision=highest)
    cross = jnp.einsum('hbv,hbk->hvk', value_rows * weight, key_rows, precision=highest)
    return (last_value.astype(jnp.float32), gram, cross)

def span_solve(query_rows, key_rows, value_rows, segment, prefix, ridge_weight):
    prev_last, gram_in, cross_in = prefix
    segment_value = segment.astype(jnp.float32)
    carried = (segment_value == prev_last).astype(jnp.float32)[None, :, None]
    position = jnp.arange(segment.shape[0])
    within = jnp.logical_and(position[:, None] >= position[None, :], segment[:, None] == segment[None, :]).astype(jnp.float32)[None]

    def apply_gram(search):
        from_state = jnp.einsum('hbf,hef->hbe', search, gram_in, precision=highest) * carried
        scores = jnp.einsum('hte,hse->hts', search, key_rows, precision=highest) * within
        local_part = jnp.einsum('hts,hse->hte', scores, key_rows, precision=highest)
        return from_state + local_part + ridge_weight[:, None, None] * search
    solved = jnp.zeros_like(query_rows)
    remain = query_rows
    search = query_rows
    remain_square = lax.optimization_barrier(jnp.sum(remain * remain, -1, keepdims=True))
    for _ in range(CG_ITERS):
        applied = apply_gram(search)
        stepsize = remain_square / lax.optimization_barrier(jnp.sum(search * applied, -1, keepdims=True))
        solved = solved + stepsize * search
        remain = remain - stepsize * applied
        next_square = lax.optimization_barrier(jnp.sum(remain * remain, -1, keepdims=True))
        search = remain + next_square / remain_square * search
        remain_square = next_square
    from_state = jnp.einsum('hbk,hvk->hbv', solved, cross_in, precision=highest) * carried
    scores = jnp.einsum('hte,hse->hts', solved, key_rows, precision=highest) * within
    return from_state + jnp.einsum('hts,hsv->htv', scores, value_rows, precision=highest)

def reference(queries, key_vectors, value_vectors, segment_ids, ridge_weight):
    head_count = ridge_weight.shape[0]
    head_width = queries.shape[1] // head_count
    block_count = queries.shape[0] // block_rows

    def blocks(values_in):
        return values_in.reshape(block_count, block_rows, head_count, head_width)

    def advance(carried_state, inputs):
        query_block, key_block, value_block, segment = inputs
        query_rows = normed(query_block).transpose(1, 0, 2)
        key_rows = normed(key_block).transpose(1, 0, 2)
        value_rows = value_block.astype(jnp.float32).transpose(1, 0, 2)
        result = span_solve(query_rows, key_rows, value_rows, segment, carried_state, ridge_weight)
        updated = combine(carried_state, summarize(key_rows, value_rows, segment))
        return (updated, result.transpose(1, 0, 2))
    zeros_state = jnp.zeros((head_count, head_width, head_width), jnp.float32)
    start = (jnp.float32(-1.0), zeros_state, zeros_state)
    _, results = lax.scan(advance, start, (blocks(queries), blocks(key_vectors), blocks(value_vectors), segment_ids.reshape(block_count, block_rows)))
    return results.reshape(queries.shape[0], head_count * head_width)
```

```python
import jax
import jax.numpy as jnp
from jax import lax
from jax.experimental import pallas as pl
from jax.experimental.pallas import tpu as pltpu
from jax.sharding import PartitionSpec as P

CG_ITERS = 3
HEADS = 16
WIDTH = 128
ROWS = 128
HALF = ROWS // 2
INFO = 8
PART = HALF + INFO
INNER = 16
OUTER = 8
SIDE = 4
MESH = pl.DeviceIdType.MESH
F32 = jnp.float32
BF16 = jnp.bfloat16


def halves(value):
    high = value.astype(BF16)
    return high, (value - high.astype(F32)).astype(BF16)


def mm(left, right):
    return jnp.dot(left, right, preferred_element_type=F32)


def mm_split(value, stacked):
    return mm(jnp.concatenate(halves(value), 1), stacked)


def twice(value):
    return jnp.concatenate([value, value], 0)


def kernel(
    q_ref,
    k_ref,
    v_ref,
    seg_ref,
    ridge_ref,
    out_ref,
    key_t,
    scales,
    send_g,
    recv_g,
    send_c,
    recv_c,
    total_g,
    early_g,
    total_c,
    early_c,
    back_g,
    prefix_g,
    back_c,
    prefix_c,
    solved,
    send_sem,
    recv_sem,
    total_send_sem,
    total_recv_sem,
):
    group, me = lax.axis_index("outer"), lax.axis_index("inner")
    me_z, me_x = me // SIDE, lax.rem(me, SIDE)

    def peer_at(step):
        x = lax.rem(me_x + lax.rem(step, SIDE), SIDE)
        z = lax.rem(me_z + step // SIDE, SIDE)
        return z * SIDE + x

    def group_at(step):
        return lax.rem(group + OUTER + step, OUTER)

    barrier = pltpu.get_barrier_semaphore()

    def greet(step, carry):
        pl.semaphore_signal(barrier, inc=1, device_id=(group, peer_at(step)), device_id_type=MESH)
        return carry

    lax.fori_loop(1, INNER, greet, 0)
    for step in (-2, -1, 1, 2):
        pl.semaphore_signal(barrier, inc=1, device_id=(group_at(step), me), device_id_type=MESH)

    def exchange(kind, source, target, peer):
        return pltpu.make_async_remote_copy(
            src_ref=source.at[peer],
            dst_ref=target.at[me],
            send_sem=send_sem.at[kind, peer],
            recv_sem=recv_sem.at[kind, me],
            device_id=(group, peer),
            device_id_type=MESH,
        )

    def arrival(kind, source, target, peer):
        return pltpu.make_async_remote_copy(
            src_ref=source.at[peer],
            dst_ref=target.at[peer],
            send_sem=send_sem.at[kind, peer],
            recv_sem=recv_sem.at[kind, peer],
            device_id=(group, peer),
            device_id_type=MESH,
        )

    def start_all(kind, source, target):
        def body(step, carry):
            exchange(kind, source, target, peer_at(step)).start()
            return carry

        lax.fori_loop(1, INNER, body, 0)
        target[me] = source[me]

    def wait_recv_all(kind, source, target):
        def body(step, carry):
            arrival(kind, source, target, peer_at(step)).wait_recv()
            return carry

        lax.fori_loop(1, INNER, body, 0)

    def wait_send_all(kind, source, target):
        def body(step, carry):
            arrival(kind, source, target, peer_at(step)).wait_send()
            return carry

        lax.fori_loop(1, INNER, body, 0)

    def pass_on(kind, source, target, step):
        return pltpu.make_async_remote_copy(
            src_ref=source,
            dst_ref=target.at[step - 1],
            send_sem=total_send_sem.at[kind, step - 1],
            recv_sem=total_recv_sem.at[kind, step - 1],
            device_id=(group_at(step), me),
            device_id_type=MESH,
        )

    row = lax.broadcasted_iota(jnp.int32, (ROWS, ROWS), 0)
    col = lax.broadcasted_iota(jnp.int32, (ROWS, ROWS), 1)
    info_row = lax.broadcasted_iota(jnp.int32, (INFO, WIDTH), 0)
    seg_cols = jnp.broadcast_to(seg_ref[...].astype(F32), (ROWS, ROWS))
    seg_rows = seg_cols.T
    first, last = seg_rows[0:1], seg_rows[ROWS - 1 :]
    weight = (seg_cols[0:1] == last).astype(F32)
    within = jnp.logical_and(row >= col, seg_rows == seg_cols).astype(F32)
    carried = (seg_rows == first).astype(F32)
    ids = jnp.where(info_row == 1, last, jnp.where(info_row == 2, first, 0.0))

    def head_slice(head):
        return pl.ds(pl.multiple_of(head * WIDTH, WIDTH), WIDTH)

    def gram(head):
        keys = k_ref[:, head_slice(head)]
        turned = keys.astype(F32).T
        scale = lax.rsqrt(jnp.sum(turned * turned, 0, keepdims=True) + 1e-06)
        key_t[head] = turned.astype(BF16)
        scales[head] = jnp.broadcast_to(scale, (INFO, WIDTH))
        return mm_split(turned * (weight * scale * scale), twice(keys))

    def gram_pair(pair, carry):
        one, two = gram(2 * pair), gram(2 * pair + 1)
        joined = jnp.where(row <= col, one, two)
        diagonal = jnp.sum(jnp.where(row == col, two, 0.0), 0, keepdims=True)
        info = jnp.where(info_row == 0, diagonal, ids)
        send_g[2 * pair, 0:HALF] = joined[0:HALF]
        send_g[2 * pair + 1, 0:HALF] = joined[HALF:]
        send_g[2 * pair, HALF:PART] = info
        send_g[2 * pair + 1, HALF:PART] = info
        return carry

    lax.fori_loop(0, HEADS // 2, gram_pair, 0, unroll=2)
    pl.semaphore_wait(barrier, INNER - 1 + 4)
    start_all(0, send_g, recv_g)

    def cross(head, carry):
        turned = key_t[head].astype(F32) * (weight * scales[head, 0:1])
        send_c[head] = mm_split(turned, twice(v_ref[:, head_slice(head)]))
        return carry

    lax.fori_loop(0, HEADS, cross, 0, unroll=4)
    start_all(1, send_c, recv_c)

    def last_of(shard):
        return recv_g[shard, HALF + 1 : HALF + 2]

    def first_of(shard):
        return recv_g[shard, HALF + 2 : HALF + 3]

    def total_of(received):
        final = last_of(INNER - 1)

        def body(shard, acc):
            return acc + jnp.where(last_of(shard) == final, received[shard], 0.0)

        return lax.fori_loop(0, INNER - 1, body, received[INNER - 1])

    has_one = (jnp.zeros((1, WIDTH), jnp.int32) + group) >= 1
    has_two = (jnp.zeros((1, WIDTH), jnp.int32) + group) >= 2

    def early_last(which):
        return early_g[which, HALF + 1 : HALF + 2]

    def prefixes(received, early, back):
        start_last = jnp.where(has_one, early_last(0), -1.0)
        second = jnp.where(
            jnp.logical_and(has_two, early_last(1) == start_last), early[1], 0.0
        )
        running = jnp.where(has_one, early[0], 0.0) + second

        def body(shard, carry):
            running, running_last = carry
            back[shard] = jnp.where(running_last == first_of(shard), running, 0.0)
            own_last = last_of(shard)
            return (
                received[shard] + jnp.where(running_last == own_last, running, 0.0),
                own_last,
            )

        lax.fori_loop(0, INNER, body, (running, start_last))

    wait_recv_all(0, send_g, recv_g)
    summed = total_of(recv_g)
    total_g[0:HALF] = summed[0:HALF]
    total_g[HALF:PART] = jnp.where(
        info_row == 0, summed[HALF:PART], recv_g[INNER - 1, HALF:PART]
    )
    for step in (1, 2):
        pass_on(0, total_g, early_g, step).start()
    for step in (1, 2):
        pass_on(0, total_g, early_g, step).wait_recv()
    prefixes(recv_g, early_g, back_g)
    start_all(2, back_g, prefix_g)

    wait_recv_all(1, send_c, recv_c)
    total_c[...] = total_of(recv_c)
    for step in (1, 2):
        pass_on(1, total_c, early_c, step).start()
    for step in (1, 2):
        pass_on(1, total_c, early_c, step).wait_recv()
    prefixes(recv_c, early_c, back_c)
    start_all(3, back_c, prefix_c)

    wait_recv_all(2, back_g, prefix_g)

    def solve(head, gram_in):
        cols = head_slice(head)
        keys, turned = k_ref[:, cols], key_t[head]
        scale = scales[head, 0:1]
        ridge = ridge_ref[head]
        gram_high, gram_low = halves(gram_in)
        both = twice(jnp.concatenate([gram_high, turned], 1))
        key_pair = twice(keys)
        key_mask = within * (scale * scale)
        query = q_ref[:, cols].astype(F32)
        remain = query * lax.rsqrt(jnp.sum(query * query, -1, keepdims=True) + 1e-06)
        search = remain
        remain_square = jnp.sum(remain * remain, -1, keepdims=True)
        answer = jnp.zeros_like(remain)
        for step in range(CG_ITERS):
            high, low = halves(search)
            product = mm(jnp.concatenate([high, low], 1), both)
            from_state = product[:, :WIDTH] + mm(high, gram_low)
            local = mm_split(product[:, WIDTH:] * key_mask, key_pair)
            applied = from_state * carried + local + ridge * search
            stepsize = remain_square / jnp.sum(search * applied, -1, keepdims=True)
            answer = answer + stepsize * search
            if step < CG_ITERS - 1:
                remain = remain - stepsize * applied
                next_square = jnp.sum(remain * remain, -1, keepdims=True)
                search = remain + next_square / remain_square * search
                remain_square = next_square
        scores = mm_split(answer, twice(turned)) * (within * scale)
        out_ref[:, cols] = mm_split(scores, twice(v_ref[:, cols]))
        solved[head] = answer * carried

    def solve_pair(pair, carry):
        joined = jnp.concatenate([prefix_g[2 * pair, 0:HALF], prefix_g[2 * pair + 1, 0:HALF]], 0)
        turned = joined.T
        diagonal = prefix_g[2 * pair, HALF : HALF + 1]
        one = jnp.where(row <= col, joined, turned)
        two = jnp.where(row == col, diagonal, jnp.where(row > col, joined, turned))
        solve(2 * pair, one)
        solve(2 * pair + 1, two)
        return carry

    lax.fori_loop(0, HEADS // 2, solve_pair, 0, unroll=2)

    wait_recv_all(3, back_c, prefix_c)

    def finish(head, carry):
        cols = head_slice(head)
        high, low = halves(solved[head])
        cross_high, cross_low = halves(prefix_c[head])
        out_ref[:, cols] = (
            out_ref[:, cols]
            + mm(jnp.concatenate([high, low], 1), twice(cross_high))
            + mm(high, cross_low)
        )
        return carry

    lax.fori_loop(0, HEADS, finish, 0, unroll=4)

    wait_send_all(0, send_g, recv_g)
    wait_send_all(1, send_c, recv_c)
    wait_send_all(2, back_g, prefix_g)
    wait_send_all(3, back_c, prefix_c)
    for step in (1, 2):
        pass_on(0, total_g, early_g, step).wait_send()
        pass_on(1, total_c, early_c, step).wait_send()


def on_device(queries, key_vectors, value_vectors, segment_ids, ridge_weight):
    vmem = pl.BlockSpec(memory_space=pltpu.VMEM)
    state_g = pltpu.VMEM((INNER, PART, WIDTH), F32)
    state_c = pltpu.VMEM((INNER, ROWS, WIDTH), F32)
    return pl.pallas_call(
        kernel,
        name="mesa",
        out_shape=jax.ShapeDtypeStruct((ROWS, HEADS * WIDTH), F32),
        in_specs=[vmem, vmem, vmem, vmem, pl.BlockSpec(memory_space=pltpu.SMEM)],
        out_specs=vmem,
        scratch_shapes=[
            pltpu.VMEM((HEADS, WIDTH, ROWS), BF16),
            pltpu.VMEM((HEADS, INFO, WIDTH), F32),
            state_g,
            state_g,
            state_c,
            state_c,
            pltpu.VMEM((PART, WIDTH), F32),
            pltpu.VMEM((2, PART, WIDTH), F32),
            pltpu.VMEM((ROWS, WIDTH), F32),
            pltpu.VMEM((2, ROWS, WIDTH), F32),
            state_g,
            state_g,
            state_c,
            state_c,
            pltpu.VMEM((HEADS, ROWS, WIDTH), F32),
            pltpu.SemaphoreType.DMA((4, INNER)),
            pltpu.SemaphoreType.DMA((4, INNER)),
            pltpu.SemaphoreType.DMA((2, 2)),
            pltpu.SemaphoreType.DMA((2, 2)),
        ],
        compiler_params=pltpu.CompilerParams(
            collective_id=0, has_side_effects=True, vmem_limit_bytes=48 << 20
        ),
    )(
        queries,
        key_vectors,
        value_vectors,
        segment_ids.reshape(1, ROWS),
        ridge_weight,
    )


def solution(mesh):
    spec = P(("outer", "inner"), None)
    return jax.shard_map(
        on_device,
        mesh=mesh,
        in_specs=(spec, spec, spec, P(("outer", "inner")), P()),
        out_specs=spec,
        check_vma=False,
    )
```

```python
import jax
import jax.numpy as jnp
from jax import lax
from jax.experimental import pallas as pl
from jax.experimental.pallas import tpu as pltpu
from jax.sharding import PartitionSpec as P

CG_ITERS = 3
HEADS = 16
WIDTH = 128
ROWS = 128
HALF = ROWS // 2
INFO = 8
PART = HALF + INFO
INNER = 16
OUTER = 8
SIDE = 4
GROUP = 4
OFFSETS = sorted(
    ((x, z) for z in range(SIDE) for x in range(SIDE) if (x, z) != (0, 0)),
    key=lambda o: -(min(o[0], SIDE - o[0]) + min(o[1], SIDE - o[1])),
)
MESH = pl.DeviceIdType.MESH
F32 = jnp.float32
BF16 = jnp.bfloat16


def halves(value):
    high = value.astype(BF16)
    return high, (value - high.astype(F32)).astype(BF16)


def mm(left, right):
    return jnp.dot(left, right, preferred_element_type=F32)


def mm_split(value, stacked):
    return mm(jnp.concatenate(halves(value), 1), stacked)


def twice(value):
    return jnp.concatenate([value, value], 0)


def twice_wide(value):
    return jnp.concatenate([value, value], 1)


def kernel(
    q_hbm,
    k_hbm,
    v_hbm,
    seg_ref,
    ridge_ref,
    out_ref,
    q_ref,
    k_ref,
    v_ref,
    key_t,
    scales,
    masks,
    query_t,
    first_local,
    send_g,
    recv_g,
    send_c,
    recv_c,
    total_g,
    early_g,
    total_c,
    early_c,
    back_g,
    prefix_g,
    back_c,
    prefix_c,
    solved,
    load_sem,
    send_sem,
    recv_sem,
    total_send_sem,
    total_recv_sem,
):
    group, me = lax.axis_index("outer"), lax.axis_index("inner")
    me_z, me_x = me // SIDE, lax.rem(me, SIDE)
    peers = [
        lax.rem(me_z + z, SIDE) * SIDE + lax.rem(me_x + x, SIDE) for x, z in OFFSETS
    ]

    def group_at(step):
        return lax.rem(group + OUTER + step, OUTER)

    loads = [
        pltpu.make_async_copy(source, target, load_sem.at[place])
        for place, (source, target) in enumerate(
            ((k_hbm, k_ref), (v_hbm, v_ref), (q_hbm, q_ref))
        )
    ]
    for load in loads:
        load.start()

    barrier = pltpu.get_barrier_semaphore()
    for peer in peers:
        pl.semaphore_signal(barrier, inc=1, device_id=(group, peer), device_id_type=MESH)
    for step in (-2, -1, 1, 2):
        pl.semaphore_signal(barrier, inc=1, device_id=(group_at(step), me), device_id_type=MESH)

    def start_all(kind, source, target, rows):
        for peer in peers:
            pltpu.make_async_remote_copy(
                src_ref=source.at[peer, rows],
                dst_ref=target.at[me, rows],
                send_sem=send_sem.at[kind],
                recv_sem=recv_sem.at[kind],
                device_id=(group, peer),
                device_id_type=MESH,
            ).start()
        target[me, rows] = source[me, rows]

    def all_of(kind, source, target, rows):
        blocks = pl.ds(0, INNER - 1)
        return pltpu.make_async_remote_copy(
            src_ref=source.at[blocks, rows],
            dst_ref=target.at[blocks, rows],
            send_sem=send_sem.at[kind],
            recv_sem=recv_sem.at[kind],
            device_id=(group, peers[0]),
            device_id_type=MESH,
        )

    def pass_on(kind, source, target, step, rows):
        return pltpu.make_async_remote_copy(
            src_ref=source.at[rows],
            dst_ref=target.at[step - 1, rows],
            send_sem=total_send_sem.at[kind, step - 1],
            recv_sem=total_recv_sem.at[kind, step - 1],
            device_id=(group_at(step), me),
            device_id_type=MESH,
        )

    row = lax.broadcasted_iota(jnp.int32, (ROWS, ROWS), 0)
    col = lax.broadcasted_iota(jnp.int32, (ROWS, ROWS), 1)
    info_row = lax.broadcasted_iota(jnp.int32, (INFO, WIDTH), 0)
    seg_cols = jnp.broadcast_to(seg_ref[...].astype(F32), (ROWS, ROWS))
    seg_rows = seg_cols.T
    first, last = seg_rows[0:1], seg_rows[ROWS - 1 :]
    weight = (seg_cols[0:1] == last).astype(F32)
    same = seg_rows == seg_cols
    within = jnp.logical_and(row >= col, same).astype(F32)
    within_t = jnp.logical_and(col >= row, same).astype(F32)
    carried_t = (seg_cols[0:1] == first).astype(F32)
    ids = jnp.where(info_row == 1, last, jnp.where(info_row == 2, first, 0.0))
    whole, lower, upper = pl.ds(0, PART), pl.ds(0, HALF), pl.ds(HALF, HALF)

    def head_slice(head):
        return pl.ds(pl.multiple_of(head * WIDTH, WIDTH), WIDTH)

    def gram(head):
        keys = k_ref[:, head_slice(head)]
        turned = keys.astype(F32).T
        scale = lax.rsqrt(jnp.sum(turned * turned, 0, keepdims=True) + 1e-06)
        key_t[head] = turned.astype(BF16)
        scales[head] = jnp.broadcast_to(scale, (INFO, WIDTH))
        return mm_split(turned * (weight * scale * scale), twice(keys))

    def gram_pair(pair, carry):
        one, two = gram(2 * pair), gram(2 * pair + 1)
        joined = jnp.where(row <= col, one, two)
        diagonal = jnp.sum(jnp.where(row == col, two, 0.0), 0, keepdims=True)
        info = jnp.where(info_row == 0, diagonal, ids)
        send_g[2 * pair, 0:HALF] = joined[0:HALF]
        send_g[2 * pair + 1, 0:HALF] = joined[HALF:]
        send_g[2 * pair, HALF:PART] = info
        send_g[2 * pair + 1, HALF:PART] = info
        return carry

    loads[0].wait()
    lax.fori_loop(0, HEADS // 2, gram_pair, 0, unroll=2)
    pl.semaphore_wait(barrier, INNER - 1 + 4)
    start_all(0, send_g, recv_g, whole)

    def cross(head, carry):
        turned = key_t[head].astype(F32) * (weight * scales[head, 0:1])
        send_c[head] = mm_split(turned, twice(v_ref[:, head_slice(head)]))
        return carry

    loads[1].wait()
    lax.fori_loop(0, HEADS, cross, 0, unroll=4)
    start_all(1, send_c, recv_c, lower)
    start_all(2, send_c, recv_c, upper)

    def prepare(head, carry):
        cols = head_slice(head)
        keys = k_ref[:, cols]
        widened = keys.astype(F32)
        scale = lax.rsqrt(jnp.sum(widened * widened, -1, keepdims=True) + 1e-06)
        mask = within_t * (scale * scale)
        masks[head] = mask
        query = q_ref[:, cols].astype(F32).T
        query = query * lax.rsqrt(jnp.sum(query * query, 0, keepdims=True) + 1e-06)
        query_t[head] = query
        scores = mm(twice_wide(keys), jnp.concatenate(halves(query), 0)) * mask
        local = mm(twice_wide(key_t[head]), jnp.concatenate(halves(scores), 0))
        first_local[head] = local + ridge_ref[head] * query
        return carry

    loads[2].wait()
    lax.fori_loop(0, HEADS, prepare, 0, unroll=4)

    def last_of(shard):
        return recv_g[shard, HALF + 1 : HALF + 2]

    def first_of(shard):
        return recv_g[shard, HALF + 2 : HALF + 3]

    def total_of(received, rows):
        final = last_of(INNER - 1)
        summed = received[INNER - 1, rows]
        for shard in range(INNER - 1):
            summed = summed + jnp.where(last_of(shard) == final, received[shard, rows], 0.0)
        return summed

    has_one = (jnp.zeros((1, WIDTH), jnp.int32) + group) >= 1
    has_two = (jnp.zeros((1, WIDTH), jnp.int32) + group) >= 2

    def early_last(which):
        return early_g[which, HALF + 1 : HALF + 2]

    def prefixes(received, early, back, rows):
        running_last = jnp.where(has_one, early_last(0), -1.0)
        second = jnp.where(
            jnp.logical_and(has_two, early_last(1) == running_last), early[1, rows], 0.0
        )
        running = jnp.where(has_one, early[0, rows], 0.0) + second
        for shard in range(INNER):
            back[shard, rows] = jnp.where(running_last == first_of(shard), running, 0.0)
            own_last = last_of(shard)
            running = received[shard, rows] + jnp.where(running_last == own_last, running, 0.0)
            running_last = own_last

    def hand_on(kind, source, target, rows):
        for step in (1, 2):
            pass_on(kind, source, target, step, rows).start()

    def take(kind, source, target, rows):
        for step in (1, 2):
            pass_on(kind, source, target, step, rows).wait_recv()

    all_of(0, send_g, recv_g, whole).wait_recv()
    summed = total_of(recv_g, whole)
    total_g[0:HALF] = summed[0:HALF]
    total_g[HALF:PART] = jnp.where(
        info_row == 0, summed[HALF:PART], recv_g[INNER - 1, HALF:PART]
    )
    hand_on(0, total_g, early_g, whole)
    take(0, total_g, early_g, whole)
    prefixes(recv_g, early_g, back_g, whole)
    start_all(3, back_g, prefix_g, whole)

    for kind, rows in ((1, lower), (2, upper)):
        all_of(kind, send_c, recv_c, rows).wait_recv()
        total_c[rows] = total_of(recv_c, rows)
        hand_on(kind, total_c, early_c, rows)
        take(kind, total_c, early_c, rows)
        prefixes(recv_c, early_c, back_c, rows)
        start_all(kind + 3, back_c, prefix_c, rows)

    all_of(3, back_g, prefix_g, whole).wait_recv()

    def solve(heads, grams):
        mats, pairs, searches, remains, squares, answers = [], [], [], [], [], []
        for head, gram_in in zip(heads, grams):
            keys = k_ref[:, head_slice(head)]
            mats.append(twice_wide(jnp.concatenate([*halves(gram_in), keys], 0)))
            pairs.append(twice_wide(key_t[head]))
            query = query_t[head]
            searches.append(query)
            remains.append(query)
            squares.append(jnp.sum(query * query, 0, keepdims=True))
            answers.append(None)
        count = range(len(heads))
        for step in range(CG_ITERS):
            stacks = [jnp.concatenate(halves(searches[n]), 0) for n in count]
            if step == 0:
                products = [mm(mats[n][: 2 * WIDTH], stacks[n]) for n in count]
                locals_ = [first_local[heads[n]] for n in count]
            else:
                products = [mm(mats[n], stacks[n]) for n in count]
                scores = [products[n][2 * WIDTH :] * masks[heads[n]] for n in count]
                locals_ = [
                    mm(pairs[n], jnp.concatenate(halves(scores[n]), 0))
                    + ridge_ref[heads[n]] * searches[n]
                    for n in count
                ]
            applied = [
                (products[n][:WIDTH] + products[n][WIDTH : 2 * WIDTH]) * carried_t + locals_[n]
                for n in count
            ]
            sizes = [
                squares[n] / jnp.sum(searches[n] * applied[n], 0, keepdims=True) for n in count
            ]
            for n in count:
                move = sizes[n] * searches[n]
                answers[n] = move if step == 0 else answers[n] + move
            if step < CG_ITERS - 1:
                remains = [remains[n] - sizes[n] * applied[n] for n in count]
                nexts = [jnp.sum(remains[n] * remains[n], 0, keepdims=True) for n in count]
                searches = [
                    remains[n] + (nexts[n] / squares[n]) * searches[n] for n in count
                ]
                squares = nexts
        for n in count:
            head = heads[n]
            solved[head] = answers[n].T

    def solve_some(some, carry):
        heads, grams = [], []
        for offset in range(GROUP // 2):
            pair = some * (GROUP // 2) + offset
            joined = jnp.concatenate(
                [prefix_g[2 * pair, 0:HALF], prefix_g[2 * pair + 1, 0:HALF]], 0
            )
            turned = joined.T
            diagonal = prefix_g[2 * pair, HALF : HALF + 1]
            grams.append(jnp.where(row <= col, joined, turned))
            grams.append(
                jnp.where(row == col, diagonal, jnp.where(row > col, joined, turned))
            )
            heads += [2 * pair, 2 * pair + 1]
        solve(heads, grams)
        return carry

    lax.fori_loop(0, HEADS // GROUP, solve_some, 0)

    def read_out(head, carry):
        cols = head_slice(head)
        scale = scales[head, 0:1]
        scores = mm_split(solved[head], twice(key_t[head])) * (within * scale)
        out_ref[:, cols] = mm_split(scores, twice(v_ref[:, cols]))
        return carry

    lax.fori_loop(0, HEADS, read_out, 0, unroll=4)
    carried = (seg_rows == first).astype(F32)

    def add_cross(rows):
        def body(head, carry):
            cols = head_slice(head)
            high, low = halves(solved[head] * carried)
            high, low = high[:, rows.start : rows.start + HALF], low[:, rows.start : rows.start + HALF]
            cross_high, cross_low = halves(prefix_c[head, rows])
            stacked = jnp.concatenate([cross_high, cross_high, cross_low], 0)
            out_ref[:, cols] = out_ref[:, cols] + mm(
                jnp.concatenate([high, low, high], 1), stacked
            )
            return carry

        lax.fori_loop(0, HEADS, body, 0, unroll=4)

    all_of(0, send_g, recv_g, whole).wait_send()
    for kind, rows in ((1, lower), (2, upper)):
        all_of(kind, send_c, recv_c, rows).wait_send()
    all_of(3, back_g, prefix_g, whole).wait_send()
    for step in (1, 2):
        pass_on(0, total_g, early_g, step, whole).wait_send()
        pass_on(1, total_c, early_c, step, lower).wait_send()
        pass_on(2, total_c, early_c, step, upper).wait_send()
    all_of(4, back_c, prefix_c, lower).wait_recv()
    add_cross(lower)
    all_of(4, back_c, prefix_c, lower).wait_send()
    all_of(5, back_c, prefix_c, upper).wait_recv()
    add_cross(upper)
    all_of(5, back_c, prefix_c, upper).wait_send()


def on_device(queries, key_vectors, value_vectors, segment_ids, ridge_weight):
    vmem = pl.BlockSpec(memory_space=pltpu.VMEM)
    hbm = pl.BlockSpec(memory_space=pltpu.HBM)
    operand = pltpu.VMEM((ROWS, HEADS * WIDTH), BF16)
    state_g = pltpu.VMEM((INNER, PART, WIDTH), F32)
    state_c = pltpu.VMEM((INNER, ROWS, WIDTH), F32)
    return pl.pallas_call(
        kernel,
        name="mesa",
        out_shape=jax.ShapeDtypeStruct((ROWS, HEADS * WIDTH), F32),
        in_specs=[hbm, hbm, hbm, vmem, pl.BlockSpec(memory_space=pltpu.SMEM)],
        out_specs=vmem,
        scratch_shapes=[
            operand,
            operand,
            operand,
            pltpu.VMEM((HEADS, WIDTH, ROWS), BF16),
            pltpu.VMEM((HEADS, INFO, WIDTH), F32),
            state_c,
            state_c,
            state_c,
            state_g,
            state_g,
            state_c,
            state_c,
            pltpu.VMEM((PART, WIDTH), F32),
            pltpu.VMEM((2, PART, WIDTH), F32),
            pltpu.VMEM((ROWS, WIDTH), F32),
            pltpu.VMEM((2, ROWS, WIDTH), F32),
            state_g,
            state_g,
            state_c,
            state_c,
            state_c,
            pltpu.SemaphoreType.DMA((3,)),
            pltpu.SemaphoreType.DMA((6,)),
            pltpu.SemaphoreType.DMA((6,)),
            pltpu.SemaphoreType.DMA((3, 2)),
            pltpu.SemaphoreType.DMA((3, 2)),
        ],
        compiler_params=pltpu.CompilerParams(
            collective_id=0, has_side_effects=True, vmem_limit_bytes=48 << 20
        ),
    )(
        queries,
        key_vectors,
        value_vectors,
        segment_ids.reshape(1, ROWS),
        ridge_weight,
    )


def solution(mesh):
    spec = P(("outer", "inner"), None)
    return jax.shard_map(
        on_device,
        mesh=mesh,
        in_specs=(spec, spec, spec, P(("outer", "inner")), P()),
        out_specs=spec,
        check_vma=False,
    )
```

```python
import jax
import jax.numpy as jnp
from jax import lax
from jax.experimental import pallas as pl
from jax.experimental.pallas import tpu as pltpu
from jax.sharding import PartitionSpec as P

CG_ITERS = 3
HEADS = 16
WIDTH = 128
ROWS = 128
HALF = ROWS // 2
INFO = 8
PART = HALF + INFO
INNER = 16
OUTER = 8
SIDE = 4
GROUP = 4
LAST = 5
OFFSETS = sorted(
    ((x, z) for z in range(SIDE) for x in range(SIDE) if (x, z) != (0, 0)),
    key=lambda o: -(min(o[0], SIDE - o[0]) + min(o[1], SIDE - o[1])),
)
MESH = pl.DeviceIdType.MESH
F32 = jnp.float32
BF16 = jnp.bfloat16


def halves(value):
    high = value.astype(BF16)
    return high, (value - high.astype(F32)).astype(BF16)


def mm(left, right):
    return jnp.dot(left, right, preferred_element_type=F32)


def mm_split(value, stacked):
    return mm(jnp.concatenate(halves(value), 1), stacked)


def twice(value):
    return jnp.concatenate([value, value], 0)


def twice_wide(value):
    return jnp.concatenate([value, value], 1)


def kernel(
    q_hbm,
    k_hbm,
    v_hbm,
    seg_hbm,
    ridge_hbm,
    out_ref,
    q_ref,
    k_ref,
    v_ref,
    seg_ref,
    ridge_ref,
    key_t,
    scales,
    masks,
    query_t,
    first_local,
    send_g,
    recv_g,
    send_c,
    recv_c,
    total_g,
    early_g,
    total_c,
    early_c,
    back_g,
    prefix_g,
    back_c,
    prefix_c,
    solved,
    load_sem,
    send_sem,
    recv_sem,
    total_send_sem,
    total_recv_sem,
):
    group, me = lax.axis_index("outer"), lax.axis_index("inner")
    me_z, me_x = me // SIDE, lax.rem(me, SIDE)
    peers = [
        lax.rem(me_z + z, SIDE) * SIDE + lax.rem(me_x + x, SIDE) for x, z in OFFSETS
    ]

    def group_at(step):
        return lax.rem(group + OUTER + step, OUTER)

    loads = [
        pltpu.make_async_copy(source, target, load_sem.at[place])
        for place, (source, target) in enumerate(
            (
                (seg_hbm, seg_ref),
                (k_hbm, k_ref),
                (v_hbm, v_ref),
                (q_hbm, q_ref),
                (ridge_hbm, ridge_ref),
            )
        )
    ]
    for load in loads:
        load.start()

    barrier = pltpu.get_barrier_semaphore()
    for peer in peers:
        pl.semaphore_signal(barrier, inc=1, device_id=(group, peer), device_id_type=MESH)
    for step in (-2, -1, 1, 2):
        pl.semaphore_signal(barrier, inc=1, device_id=(group_at(step), me), device_id_type=MESH)

    ranked = [place + (place >= me).astype(jnp.int32) for place in range(INNER - 1)]

    def start_all(kind, source, target, rows, order):
        for peer in order:
            pltpu.make_async_remote_copy(
                src_ref=source.at[peer, rows],
                dst_ref=target.at[me, rows],
                send_sem=send_sem.at[kind],
                recv_sem=recv_sem.at[kind],
                device_id=(group, peer),
                device_id_type=MESH,
            ).start()
        target[me, rows] = source[me, rows]

    def all_of(kind, source, target, rows):
        blocks = pl.ds(0, INNER - 1)
        return pltpu.make_async_remote_copy(
            src_ref=source.at[blocks, rows],
            dst_ref=target.at[blocks, rows],
            send_sem=send_sem.at[kind],
            recv_sem=recv_sem.at[kind],
            device_id=(group, peers[0]),
            device_id_type=MESH,
        )

    def pass_on(kind, source, target, step, rows):
        return pltpu.make_async_remote_copy(
            src_ref=source.at[rows],
            dst_ref=target.at[step - 1, rows],
            send_sem=total_send_sem.at[kind, step - 1],
            recv_sem=total_recv_sem.at[kind, step - 1],
            device_id=(group_at(step), me),
            device_id_type=MESH,
        )

    loads[0].wait()
    row = lax.broadcasted_iota(jnp.int32, (ROWS, ROWS), 0)
    col = lax.broadcasted_iota(jnp.int32, (ROWS, ROWS), 1)
    info_row = lax.broadcasted_iota(jnp.int32, (INFO, WIDTH), 0)
    seg_cols = jnp.broadcast_to(seg_ref[...].astype(F32), (ROWS, ROWS))
    seg_rows = seg_cols.T
    first, last = seg_rows[0:1], seg_rows[ROWS - 1 :]
    weight = (seg_cols[0:1] == last).astype(F32)
    same = seg_rows == seg_cols
    within = jnp.logical_and(row >= col, same).astype(F32)
    within_t = jnp.logical_and(col >= row, same).astype(F32)
    carried_t = (seg_cols[0:1] == first).astype(F32)
    ids = jnp.where(info_row == 1, last, jnp.where(info_row == 2, first, 0.0))
    whole, lower, upper = pl.ds(0, PART), pl.ds(0, HALF), pl.ds(HALF, HALF)
    sent = pl.ds(0, HALF + 3)
    returned = pl.ds(0, HALF + 1)

    def head_slice(head):
        return pl.ds(pl.multiple_of(head * WIDTH, WIDTH), WIDTH)

    def gram(head):
        keys = k_ref[:, head_slice(head)]
        turned = keys.astype(F32).T
        scale = lax.rsqrt(jnp.sum(turned * turned, 0, keepdims=True) + 1e-06)
        key_t[head] = turned.astype(BF16)
        scales[head] = jnp.broadcast_to(scale, (INFO, WIDTH))
        return mm_split(turned * (weight * scale * scale), twice(keys))

    def gram_pair(pair, carry):
        one, two = gram(2 * pair), gram(2 * pair + 1)
        joined = jnp.where(row <= col, one, two)
        diagonal = jnp.sum(jnp.where(row == col, two, 0.0), 0, keepdims=True)
        info = jnp.where(info_row == 0, diagonal, ids)
        send_g[2 * pair, 0:HALF] = joined[0:HALF]
        send_g[2 * pair + 1, 0:HALF] = joined[HALF:]
        send_g[2 * pair, HALF:PART] = info
        send_g[2 * pair + 1, HALF:PART] = info
        return carry

    loads[1].wait()
    lax.fori_loop(0, HEADS // 2, gram_pair, 0, unroll=2)
    pl.semaphore_wait(barrier, INNER - 1 + 4)
    start_all(0, send_g, recv_g, sent, peers)

    def cross(head, carry):
        turned = key_t[head].astype(F32) * (weight * scales[head, 0:1])
        send_c[head] = mm_split(turned, twice(v_ref[:, head_slice(head)]))
        return carry

    loads[2].wait()
    lax.fori_loop(0, HEADS, cross, 0, unroll=4)
    start_all(1, send_c, recv_c, lower, peers)
    start_all(2, send_c, recv_c, upper, peers)

    def prepare(head, carry):
        cols = head_slice(head)
        keys = k_ref[:, cols]
        widened = keys.astype(F32)
        scale = lax.rsqrt(jnp.sum(widened * widened, -1, keepdims=True) + 1e-06)
        mask = within_t * (scale * scale)
        masks[head] = mask
        query = q_ref[:, cols].astype(F32).T
        query = query * lax.rsqrt(jnp.sum(query * query, 0, keepdims=True) + 1e-06)
        query_t[head] = query
        scores = mm(twice_wide(keys), jnp.concatenate(halves(query), 0)) * mask
        local = mm(twice_wide(key_t[head]), jnp.concatenate(halves(scores), 0))
        first_local[head] = local + ridge_ref[head] * query
        return carry

    loads[3].wait()
    loads[4].wait()
    lax.fori_loop(0, HEADS, prepare, 0, unroll=4)

    def last_of(shard):
        return recv_g[shard, HALF + 1 : HALF + 2]

    def first_of(shard):
        return recv_g[shard, HALF + 2 : HALF + 3]

    def total_of(received, rows):
        final = last_of(INNER - 1)
        summed = received[INNER - 1, rows]
        for shard in range(INNER - 1):
            summed = summed + jnp.where(last_of(shard) == final, received[shard, rows], 0.0)
        return summed

    has_one = (jnp.zeros((1, WIDTH), jnp.int32) + group) >= 1
    has_two = (jnp.zeros((1, WIDTH), jnp.int32) + group) >= 2

    def early_last(which):
        return early_g[which, HALF + 1 : HALF + 2]

    def prefixes(received, early, back, rows):
        running_last = jnp.where(has_one, early_last(0), -1.0)
        second = jnp.where(
            jnp.logical_and(has_two, early_last(1) == running_last), early[1, rows], 0.0
        )
        running = jnp.where(has_one, early[0, rows], 0.0) + second
        for shard in range(INNER):
            back[shard, rows] = jnp.where(running_last == first_of(shard), running, 0.0)
            own_last = last_of(shard)
            running = received[shard, rows] + jnp.where(running_last == own_last, running, 0.0)
            running_last = own_last

    def hand_on(kind, source, target, rows):
        for step in (1, 2):
            pass_on(kind, source, target, step, rows).start()

    def take(kind, source, target, rows):
        for step in (1, 2):
            pass_on(kind, source, target, step, rows).wait_recv()

    all_of(0, send_g, recv_g, sent).wait_recv()
    summed = total_of(recv_g, whole)
    total_g[0:HALF] = summed[0:HALF]
    total_g[HALF:PART] = jnp.where(
        info_row == 0, summed[HALF:PART], recv_g[INNER - 1, HALF:PART]
    )
    hand_on(0, total_g, early_g, sent)
    take(0, total_g, early_g, sent)
    prefixes(recv_g, early_g, back_g, whole)
    start_all(3, back_g, prefix_g, returned, peers)

    for kind, rows in ((1, lower), (2, upper)):
        all_of(kind, send_c, recv_c, rows).wait_recv()
        total_c[rows] = total_of(recv_c, rows)
        hand_on(kind, total_c, early_c, rows)
        take(kind, total_c, early_c, rows)
        prefixes(recv_c, early_c, back_c, rows)
        start_all(kind + 3, back_c, prefix_c, rows, peers if kind == 1 else peers)

    all_of(3, back_g, prefix_g, returned).wait_recv()

    def solve(heads, grams):
        mats, pairs, searches, remains, squares, answers = [], [], [], [], [], []
        for head, gram_in in zip(heads, grams):
            keys = k_ref[:, head_slice(head)]
            mats.append(twice_wide(jnp.concatenate([*halves(gram_in), keys], 0)))
            pairs.append(twice_wide(key_t[head]))
            query = query_t[head]
            searches.append(query)
            remains.append(query)
            squares.append(jnp.sum(query * query, 0, keepdims=True))
            answers.append(None)
        count = range(len(heads))
        for step in range(CG_ITERS):
            stacks = [jnp.concatenate(halves(searches[n]), 0) for n in count]
            if step == 0:
                products = [mm(mats[n][: 2 * WIDTH], stacks[n]) for n in count]
                locals_ = [first_local[heads[n]] for n in count]
            else:
                products = [mm(mats[n], stacks[n]) for n in count]
                scores = [products[n][2 * WIDTH :] * masks[heads[n]] for n in count]
                locals_ = [
                    mm(pairs[n], jnp.concatenate(halves(scores[n]), 0))
                    + ridge_ref[heads[n]] * searches[n]
                    for n in count
                ]
            applied = [
                (products[n][:WIDTH] + products[n][WIDTH : 2 * WIDTH]) * carried_t + locals_[n]
                for n in count
            ]
            sizes = [
                squares[n] / jnp.sum(searches[n] * applied[n], 0, keepdims=True) for n in count
            ]
            for n in count:
                move = sizes[n] * searches[n]
                answers[n] = move if step == 0 else answers[n] + move
            if step < CG_ITERS - 1:
                remains = [remains[n] - sizes[n] * applied[n] for n in count]
                nexts = [jnp.sum(remains[n] * remains[n], 0, keepdims=True) for n in count]
                searches = [
                    remains[n] + (nexts[n] / squares[n]) * searches[n] for n in count
                ]
                squares = nexts
        for n in count:
            head = heads[n]
            solved[head] = answers[n].T

    def solve_some(some, carry):
        heads, grams = [], []
        for offset in range(GROUP // 2):
            pair = some * (GROUP // 2) + offset
            joined = jnp.concatenate(
                [prefix_g[2 * pair, 0:HALF], prefix_g[2 * pair + 1, 0:HALF]], 0
            )
            turned = joined.T
            diagonal = prefix_g[2 * pair, HALF : HALF + 1]
            grams.append(jnp.where(row <= col, joined, turned))
            grams.append(
                jnp.where(row == col, diagonal, jnp.where(row > col, joined, turned))
            )
            heads += [2 * pair, 2 * pair + 1]
        solve(heads, grams)
        return carry

    lax.fori_loop(0, HEADS // GROUP, solve_some, 0)

    def read_out(head, carry):
        cols = head_slice(head)
        scale = scales[head, 0:1]
        scores = mm_split(solved[head], twice(key_t[head])) * (within * scale)
        out_ref[:, cols] = mm_split(scores, twice(v_ref[:, cols]))
        return carry

    lax.fori_loop(0, HEADS, read_out, 0, unroll=4)
    carried = (seg_rows == first).astype(F32)

    def add_cross(head, rows):
        cols = head_slice(head)
        answer = solved[head, :, rows.start : rows.start + HALF] * carried[:, :HALF]
        high, low = halves(answer)
        cross_high, cross_low = halves(prefix_c[head, rows])
        out_ref[:, cols] = out_ref[:, cols] + mm(
            jnp.concatenate([high, low, high], 1),
            jnp.concatenate([cross_high, cross_high, cross_low], 0),
        )

    def add_lower(head, carry):
        add_cross(head, lower)
        return carry

    all_of(0, send_g, recv_g, sent).wait_send()
    for kind, rows in ((1, lower), (2, upper)):
        all_of(kind, send_c, recv_c, rows).wait_send()
    all_of(3, back_g, prefix_g, returned).wait_send()
    for step in (1, 2):
        pass_on(0, total_g, early_g, step, sent).wait_send()
        pass_on(1, total_c, early_c, step, lower).wait_send()
        pass_on(2, total_c, early_c, step, upper).wait_send()
    all_of(4, back_c, prefix_c, lower).wait_recv()
    lax.fori_loop(0, HEADS, add_lower, 0, unroll=4)
    all_of(4, back_c, prefix_c, lower).wait_send()

    def add_upper(head, carry):
        add_cross(head, upper)
        return carry

    all_of(LAST, back_c, prefix_c, upper).wait_recv()
    lax.fori_loop(0, HEADS, add_upper, 0, unroll=8)
    all_of(LAST, back_c, prefix_c, upper).wait_send()


def on_device(queries, key_vectors, value_vectors, segment_ids, ridge_weight):
    vmem = pl.BlockSpec(memory_space=pltpu.VMEM)
    hbm = pl.BlockSpec(memory_space=pltpu.HBM)
    operand = pltpu.VMEM((ROWS, HEADS * WIDTH), BF16)
    state_g = pltpu.VMEM((INNER, PART, WIDTH), F32)
    state_c = pltpu.VMEM((INNER, ROWS, WIDTH), F32)
    return pl.pallas_call(
        kernel,
        name="mesa",
        out_shape=jax.ShapeDtypeStruct((ROWS, HEADS * WIDTH), F32),
        in_specs=[hbm] * 5,
        out_specs=vmem,
        scratch_shapes=[
            operand,
            operand,
            operand,
            pltpu.VMEM((1, ROWS), jnp.int32),
            pltpu.SMEM((HEADS,), F32),
            pltpu.VMEM((HEADS, WIDTH, ROWS), BF16),
            pltpu.VMEM((HEADS, INFO, WIDTH), F32),
            state_c,
            state_c,
            state_c,
            state_g,
            state_g,
            state_c,
            state_c,
            pltpu.VMEM((PART, WIDTH), F32),
            pltpu.VMEM((2, PART, WIDTH), F32),
            pltpu.VMEM((ROWS, WIDTH), F32),
            pltpu.VMEM((2, ROWS, WIDTH), F32),
            state_g,
            state_g,
            state_c,
            state_c,
            state_c,
            pltpu.SemaphoreType.DMA((5,)),
            pltpu.SemaphoreType.DMA((6,)),
            pltpu.SemaphoreType.DMA((6,)),
            pltpu.SemaphoreType.DMA((3, 2)),
            pltpu.SemaphoreType.DMA((3, 2)),
        ],
        compiler_params=pltpu.CompilerParams(
            collective_id=0, has_side_effects=True, vmem_limit_bytes=48 << 20
        ),
    )(
        *(
            pltpu.with_memory_space_constraint(value, pltpu.HBM)
            for value in (
                queries,
                key_vectors,
                value_vectors,
                segment_ids.reshape(1, ROWS),
                ridge_weight,
            )
        ),
    )


def solution(mesh):
    spec = P(("outer", "inner"), None)
    return jax.shard_map(
        on_device,
        mesh=mesh,
        in_specs=(spec, spec, spec, P(("outer", "inner")), P()),
        out_specs=spec,
        check_vma=False,
    )
```

```python
import jax
import jax.numpy as jnp
from jax import lax
from jax.experimental import pallas as pl
from jax.experimental.pallas import tpu as pltpu
from jax.sharding import PartitionSpec as P

CG_ITERS = 3
HEADS = 16
WIDTH = 128
ROWS = 128
HALF = ROWS // 2
INFO = 8
PART = HALF + INFO
INNER = 16
OUTER = 8
SIDE = 4
GROUP = 8
STEPS = 4
LAST = 5
OFFSETS = sorted(
    ((x, z) for z in range(SIDE) for x in range(SIDE) if (x, z) != (0, 0)),
    key=lambda o: -(min(o[0], SIDE - o[0]) + min(o[1], SIDE - o[1])),
)
MESH = pl.DeviceIdType.MESH
F32 = jnp.float32
BF16 = jnp.bfloat16


def halves(value):
    high = value.astype(BF16)
    return high, (value - high.astype(F32)).astype(BF16)


def mm(left, right):
    return jnp.dot(left, right, preferred_element_type=F32)


def mm_split(value, stacked):
    return mm(jnp.concatenate(halves(value), 1), stacked)


def twice(value):
    return jnp.concatenate([value, value], 0)


def twice_wide(value):
    return jnp.concatenate([value, value], 1)


def cross_part(high, low, state):
    state_high, state_low = halves(state)
    return mm(
        jnp.concatenate([high, low, high], 1),
        jnp.concatenate([state_high, state_high, state_low], 0),
    )


def finish(part_ref, late_ref, state_ref, out_hbm, done, sems):
    stores = []
    for step in range(STEPS):
        for head in range(step * HEADS // STEPS, (step + 1) * HEADS // STEPS):
            late = late_ref[head]
            cols = pl.ds(head * WIDTH, WIDTH)
            done[:, cols] = part_ref[:, cols] + cross_part(
                late[:, :HALF], late[:, HALF:], state_ref[head, HALF:]
            )
        cols = pl.ds(step * HEADS // STEPS * WIDTH, HEADS // STEPS * WIDTH)
        stores.append(
            pltpu.make_async_copy(done.at[:, cols], out_hbm.at[:, cols], sems.at[step])
        )
        stores[-1].start()
    for store in stores:
        store.wait()


def kernel(
    q_hbm,
    k_hbm,
    v_hbm,
    seg_hbm,
    ridge_hbm,
    out_ref,
    late_ref,
    prefix_c,
    q_ref,
    k_ref,
    v_ref,
    seg_ref,
    ridge_ref,
    key_t,
    scales,
    masks,
    query_t,
    first_local,
    send_g,
    recv_g,
    send_c,
    recv_c,
    total_g,
    early_g,
    total_c,
    early_c,
    back_g,
    prefix_g,
    back_c,
    solved,
    load_sem,
    send_sem,
    recv_sem,
    total_send_sem,
    total_recv_sem,
):
    group, me = lax.axis_index("outer"), lax.axis_index("inner")
    me_z, me_x = me // SIDE, lax.rem(me, SIDE)
    peers = [
        lax.rem(me_z + z, SIDE) * SIDE + lax.rem(me_x + x, SIDE) for x, z in OFFSETS
    ]

    def group_at(step):
        return lax.rem(group + OUTER + step, OUTER)

    loads = [
        pltpu.make_async_copy(source, target, load_sem.at[place])
        for place, (source, target) in enumerate(
            (
                (seg_hbm, seg_ref),
                (k_hbm, k_ref),
                (v_hbm, v_ref),
                (q_hbm, q_ref),
                (ridge_hbm, ridge_ref),
            )
        )
    ]
    for load in loads:
        load.start()

    barrier = pltpu.get_barrier_semaphore()
    for peer in peers:
        pl.semaphore_signal(barrier, inc=1, device_id=(group, peer), device_id_type=MESH)
    for step in (-2, -1, 1, 2):
        pl.semaphore_signal(barrier, inc=1, device_id=(group_at(step), me), device_id_type=MESH)

    ranked = [place + (place >= me).astype(jnp.int32) for place in range(INNER - 1)]

    def start_all(kind, source, target, rows, order):
        for peer in order:
            pltpu.make_async_remote_copy(
                src_ref=source.at[peer, rows],
                dst_ref=target.at[me, rows],
                send_sem=send_sem.at[kind],
                recv_sem=recv_sem.at[kind],
                device_id=(group, peer),
                device_id_type=MESH,
            ).start()
        target[me, rows] = source[me, rows]

    def all_of(kind, source, target, rows):
        blocks = pl.ds(0, INNER - 1)
        return pltpu.make_async_remote_copy(
            src_ref=source.at[blocks, rows],
            dst_ref=target.at[blocks, rows],
            send_sem=send_sem.at[kind],
            recv_sem=recv_sem.at[kind],
            device_id=(group, peers[0]),
            device_id_type=MESH,
        )

    def pass_on(kind, source, target, step, rows):
        return pltpu.make_async_remote_copy(
            src_ref=source.at[rows],
            dst_ref=target.at[step - 1, rows],
            send_sem=total_send_sem.at[kind, step - 1],
            recv_sem=total_recv_sem.at[kind, step - 1],
            device_id=(group_at(step), me),
            device_id_type=MESH,
        )

    loads[0].wait()
    row = lax.broadcasted_iota(jnp.int32, (ROWS, ROWS), 0)
    col = lax.broadcasted_iota(jnp.int32, (ROWS, ROWS), 1)
    info_row = lax.broadcasted_iota(jnp.int32, (INFO, WIDTH), 0)
    seg_cols = jnp.broadcast_to(seg_ref[...].astype(F32), (ROWS, ROWS))
    seg_rows = seg_cols.T
    first, last = seg_rows[0:1], seg_rows[ROWS - 1 :]
    weight = (seg_cols[0:1] == last).astype(F32)
    same = seg_rows == seg_cols
    within = jnp.logical_and(row >= col, same).astype(F32)
    within_t = jnp.logical_and(col >= row, same).astype(F32)
    carried_t = (seg_cols[0:1] == first).astype(F32)
    ids = jnp.where(info_row == 1, last, jnp.where(info_row == 2, first, 0.0))
    whole, lower, upper = pl.ds(0, PART), pl.ds(0, HALF), pl.ds(HALF, HALF)
    sent = pl.ds(0, HALF + 3)
    returned = pl.ds(0, HALF + 1)

    def head_slice(head):
        return pl.ds(pl.multiple_of(head * WIDTH, WIDTH), WIDTH)

    def gram(head):
        keys = k_ref[:, head_slice(head)]
        turned = keys.astype(F32).T
        scale = lax.rsqrt(jnp.sum(turned * turned, 0, keepdims=True) + 1e-06)
        key_t[head] = turned.astype(BF16)
        scales[head] = jnp.broadcast_to(scale, (INFO, WIDTH))
        return mm_split(turned * (weight * scale * scale), twice(keys))

    def gram_pair(pair, carry):
        one, two = gram(2 * pair), gram(2 * pair + 1)
        joined = jnp.where(row <= col, one, two)
        diagonal = jnp.sum(jnp.where(row == col, two, 0.0), 0, keepdims=True)
        info = jnp.where(info_row == 0, diagonal, ids)
        send_g[2 * pair, 0:HALF] = joined[0:HALF]
        send_g[2 * pair + 1, 0:HALF] = joined[HALF:]
        send_g[2 * pair, HALF:PART] = info
        send_g[2 * pair + 1, HALF:PART] = info
        return carry

    loads[1].wait()
    lax.fori_loop(0, HEADS // 2, gram_pair, 0, unroll=2)
    pl.semaphore_wait(barrier, INNER - 1 + 4)
    start_all(0, send_g, recv_g, sent, peers)

    def cross(head, carry):
        turned = key_t[head].astype(F32) * (weight * scales[head, 0:1])
        send_c[head] = mm_split(turned, twice(v_ref[:, head_slice(head)]))
        return carry

    loads[2].wait()
    lax.fori_loop(0, HEADS, cross, 0, unroll=4)
    start_all(1, send_c, recv_c, lower, peers)
    start_all(2, send_c, recv_c, upper, peers)

    def prepare(head, carry):
        cols = head_slice(head)
        keys = k_ref[:, cols]
        widened = keys.astype(F32)
        scale = lax.rsqrt(jnp.sum(widened * widened, -1, keepdims=True) + 1e-06)
        mask = within_t * (scale * scale)
        masks[head] = mask
        query = q_ref[:, cols].astype(F32).T
        query = query * lax.rsqrt(jnp.sum(query * query, 0, keepdims=True) + 1e-06)
        query_t[head] = query
        scores = mm(twice_wide(keys), jnp.concatenate(halves(query), 0)) * mask
        local = mm(twice_wide(key_t[head]), jnp.concatenate(halves(scores), 0))
        first_local[head] = local + ridge_ref[head] * query
        return carry

    def prepare_some(some):
        for head in range(4 * some, 4 * some + 4):
            prepare(head, 0)

    loads[3].wait()
    loads[4].wait()
    prepare_some(0)

    def last_of(shard):
        return recv_g[shard, HALF + 1 : HALF + 2]

    def first_of(shard):
        return recv_g[shard, HALF + 2 : HALF + 3]

    def total_of(received, rows):
        final = last_of(INNER - 1)
        summed = received[INNER - 1, rows]
        for shard in range(INNER - 1):
            summed = summed + jnp.where(last_of(shard) == final, received[shard, rows], 0.0)
        return summed

    has_one = (jnp.zeros((1, WIDTH), jnp.int32) + group) >= 1
    has_two = (jnp.zeros((1, WIDTH), jnp.int32) + group) >= 2

    def early_last(which):
        return early_g[which, HALF + 1 : HALF + 2]

    def prefixes(received, early, back, rows):
        running_last = jnp.where(has_one, early_last(0), -1.0)
        second = jnp.where(
            jnp.logical_and(has_two, early_last(1) == running_last), early[1, rows], 0.0
        )
        running = jnp.where(has_one, early[0, rows], 0.0) + second
        for shard in range(INNER):
            back[shard, rows] = jnp.where(running_last == first_of(shard), running, 0.0)
            own_last = last_of(shard)
            running = received[shard, rows] + jnp.where(running_last == own_last, running, 0.0)
            running_last = own_last

    def hand_on(kind, source, target, rows):
        for step in (1, 2):
            pass_on(kind, source, target, step, rows).start()

    def take(kind, source, target, rows):
        for step in (1, 2):
            pass_on(kind, source, target, step, rows).wait_recv()

    all_of(0, send_g, recv_g, sent).wait_recv()
    summed = total_of(recv_g, whole)
    total_g[0:HALF] = summed[0:HALF]
    total_g[HALF:PART] = jnp.where(
        info_row == 0, summed[HALF:PART], recv_g[INNER - 1, HALF:PART]
    )
    hand_on(0, total_g, early_g, sent)
    prepare_some(1)
    take(0, total_g, early_g, sent)
    prefixes(recv_g, early_g, back_g, whole)
    start_all(3, back_g, prefix_g, returned, peers)

    for kind, rows in ((1, lower), (2, upper)):
        all_of(kind, send_c, recv_c, rows).wait_recv()
        total_c[rows] = total_of(recv_c, rows)
        hand_on(kind, total_c, early_c, rows)
        prepare_some(kind + 1)
        take(kind, total_c, early_c, rows)
        prefixes(recv_c, early_c, back_c, rows)
        start_all(kind + 3, back_c, prefix_c, rows, peers if kind == 1 else peers)

    all_of(3, back_g, prefix_g, returned).wait_recv()

    def solve(heads, grams):
        mats, pairs, searches, remains, squares, answers = [], [], [], [], [], []
        for head, gram_in in zip(heads, grams):
            keys = k_ref[:, head_slice(head)]
            mats.append(twice_wide(jnp.concatenate([*halves(gram_in), keys], 0)))
            pairs.append(twice_wide(key_t[head]))
            query = query_t[head]
            searches.append(query)
            remains.append(query)
            squares.append(jnp.sum(query * query, 0, keepdims=True))
            answers.append(None)
        count = range(len(heads))
        for step in range(CG_ITERS):
            stacks = [jnp.concatenate(halves(searches[n]), 0) for n in count]
            if step == 0:
                products = [mm(mats[n][: 2 * WIDTH], stacks[n]) for n in count]
                locals_ = [first_local[heads[n]] for n in count]
            else:
                products = [mm(mats[n], stacks[n]) for n in count]
                scores = [products[n][2 * WIDTH :] * masks[heads[n]] for n in count]
                locals_ = [
                    mm(pairs[n], jnp.concatenate(halves(scores[n]), 0))
                    + ridge_ref[heads[n]] * searches[n]
                    for n in count
                ]
            applied = [
                (products[n][:WIDTH] + products[n][WIDTH : 2 * WIDTH]) * carried_t + locals_[n]
                for n in count
            ]
            sizes = [
                squares[n] / jnp.sum(searches[n] * applied[n], 0, keepdims=True) for n in count
            ]
            for n in count:
                move = sizes[n] * searches[n]
                answers[n] = move if step == 0 else answers[n] + move
            if step < CG_ITERS - 1:
                remains = [remains[n] - sizes[n] * applied[n] for n in count]
                nexts = [jnp.sum(remains[n] * remains[n], 0, keepdims=True) for n in count]
                searches = [
                    remains[n] + (nexts[n] / squares[n]) * searches[n] for n in count
                ]
                squares = nexts
        for n in count:
            head = heads[n]
            solved[head] = answers[n].T

    def solve_some(some, carry):
        heads, grams = [], []
        for offset in range(GROUP // 2):
            pair = some * (GROUP // 2) + offset
            joined = jnp.concatenate(
                [prefix_g[2 * pair, 0:HALF], prefix_g[2 * pair + 1, 0:HALF]], 0
            )
            turned = joined.T
            diagonal = prefix_g[2 * pair, HALF : HALF + 1]
            grams.append(jnp.where(row <= col, joined, turned))
            grams.append(
                jnp.where(row == col, diagonal, jnp.where(row > col, joined, turned))
            )
            heads += [2 * pair, 2 * pair + 1]
        solve(heads, grams)
        return carry

    lax.fori_loop(0, HEADS // GROUP, solve_some, 0)

    def read_out(head, carry):
        cols = head_slice(head)
        scale = scales[head, 0:1]
        scores = mm_split(solved[head], twice(key_t[head])) * (within * scale)
        out_ref[:, cols] = mm_split(scores, twice(v_ref[:, cols]))
        return carry

    lax.fori_loop(0, HEADS, read_out, 0, unroll=8)
    carried = (seg_rows == first).astype(F32)

    def add_lower(head, carry):
        cols = head_slice(head)
        high, low = halves(solved[head] * carried)
        late_ref[head] = jnp.concatenate([high[:, HALF:], low[:, HALF:]], 1)
        out_ref[:, cols] = out_ref[:, cols] + cross_part(
            high[:, :HALF], low[:, :HALF], prefix_c[head, lower]
        )
        return carry

    all_of(0, send_g, recv_g, sent).wait_send()
    for kind, rows in ((1, lower), (2, upper)):
        all_of(kind, send_c, recv_c, rows).wait_send()
    all_of(3, back_g, prefix_g, returned).wait_send()
    for step in (1, 2):
        pass_on(0, total_g, early_g, step, sent).wait_send()
        pass_on(1, total_c, early_c, step, lower).wait_send()
        pass_on(2, total_c, early_c, step, upper).wait_send()
    all_of(4, back_c, prefix_c, lower).wait_recv()
    lax.fori_loop(0, HEADS, add_lower, 0, unroll=8)
    all_of(4, back_c, prefix_c, lower).wait_send()

    all_of(LAST, back_c, prefix_c, upper).wait_recv()
    all_of(LAST, back_c, prefix_c, upper).wait_send()


def on_device(queries, key_vectors, value_vectors, segment_ids, ridge_weight):
    vmem = pl.BlockSpec(memory_space=pltpu.VMEM)
    hbm = pl.BlockSpec(memory_space=pltpu.HBM)
    operand = pltpu.VMEM((ROWS, HEADS * WIDTH), BF16)
    state_g = pltpu.VMEM((INNER, PART, WIDTH), F32)
    state_c = pltpu.VMEM((INNER, ROWS, WIDTH), F32)
    part, late, state = pl.pallas_call(
        kernel,
        name="mesa",
        out_shape=(
            jax.ShapeDtypeStruct((ROWS, HEADS * WIDTH), F32),
            jax.ShapeDtypeStruct((HEADS, ROWS, WIDTH), BF16),
            jax.ShapeDtypeStruct((INNER, ROWS, WIDTH), F32),
        ),
        in_specs=[hbm] * 5,
        out_specs=(vmem, vmem, vmem),
        scratch_shapes=[
            operand,
            operand,
            operand,
            pltpu.VMEM((1, ROWS), jnp.int32),
            pltpu.SMEM((HEADS,), F32),
            pltpu.VMEM((HEADS, WIDTH, ROWS), BF16),
            pltpu.VMEM((HEADS, INFO, WIDTH), F32),
            state_c,
            state_c,
            state_c,
            state_g,
            state_g,
            state_c,
            state_c,
            pltpu.VMEM((PART, WIDTH), F32),
            pltpu.VMEM((2, PART, WIDTH), F32),
            pltpu.VMEM((ROWS, WIDTH), F32),
            pltpu.VMEM((2, ROWS, WIDTH), F32),
            state_g,
            state_g,
            state_c,
            state_c,
            pltpu.SemaphoreType.DMA((5,)),
            pltpu.SemaphoreType.DMA((6,)),
            pltpu.SemaphoreType.DMA((6,)),
            pltpu.SemaphoreType.DMA((3, 2)),
            pltpu.SemaphoreType.DMA((3, 2)),
        ],
        compiler_params=pltpu.CompilerParams(
            collective_id=0, has_side_effects=True, vmem_limit_bytes=48 << 20
        ),
    )(
        *(
            pltpu.with_memory_space_constraint(value, pltpu.HBM)
            for value in (
                queries,
                key_vectors,
                value_vectors,
                segment_ids.reshape(1, ROWS),
                ridge_weight,
            )
        ),
    )
    return pl.pallas_call(
        finish,
        name="finish",
        out_shape=jax.ShapeDtypeStruct((ROWS, HEADS * WIDTH), F32),
        in_specs=[vmem, vmem, vmem],
        out_specs=hbm,
        scratch_shapes=[
            pltpu.VMEM((ROWS, HEADS * WIDTH), F32),
            pltpu.SemaphoreType.DMA((STEPS,)),
        ],
        compiler_params=pltpu.CompilerParams(vmem_limit_bytes=16 << 20),
    )(part, late, state)


def solution(mesh):
    spec = P(("outer", "inner"), None)
    return jax.shard_map(
        on_device,
        mesh=mesh,
        in_specs=(spec, spec, spec, P(("outer", "inner")), P()),
        out_specs=spec,
        check_vma=False,
    )
```

```python
import jax
import jax.numpy as jnp
from jax import lax
from jax.experimental import pallas as pl
from jax.experimental.pallas import tpu as pltpu
from jax.sharding import PartitionSpec as P

CG_ITERS = 3
HEADS = 16
WIDTH = 128
ROWS = 128
HALF = ROWS // 2
INFO = 8
PART = HALF + INFO
INNER = 16
OUTER = 8
SIDE = 4
GROUP = 8
STEPS = 4
LAST = 5
OFFSETS = sorted(
    ((x, z) for z in range(SIDE) for x in range(SIDE) if (x, z) != (0, 0)),
    key=lambda o: -(min(o[0], SIDE - o[0]) + min(o[1], SIDE - o[1])),
)
MESH = pl.DeviceIdType.MESH
F32 = jnp.float32
BF16 = jnp.bfloat16


def halves(value):
    high = value.astype(BF16)
    return high, (value - high.astype(F32)).astype(BF16)


def mm(left, right):
    return jnp.dot(left, right, preferred_element_type=F32)


def mm_split(value, stacked):
    return mm(jnp.concatenate(halves(value), 1), stacked)


def twice(value):
    return jnp.concatenate([value, value], 0)


def twice_wide(value):
    return jnp.concatenate([value, value], 1)


def cross_part(high, low, state):
    state_high, state_low = halves(state)
    return mm(
        jnp.concatenate([high, low, high], 1),
        jnp.concatenate([state_high, state_high, state_low], 0),
    )


def finish(part_ref, late_ref, state_ref, out_hbm, done, sems):
    stores = []
    for step in range(STEPS):
        for head in range(step * HEADS // STEPS, (step + 1) * HEADS // STEPS):
            late = late_ref[head]
            cols = pl.ds(head * WIDTH, WIDTH)
            done[:, cols] = part_ref[:, cols] + cross_part(
                late[:, :HALF], late[:, HALF:], state_ref[head, HALF:]
            )
        cols = pl.ds(step * HEADS // STEPS * WIDTH, HEADS // STEPS * WIDTH)
        stores.append(
            pltpu.make_async_copy(done.at[:, cols], out_hbm.at[:, cols], sems.at[step])
        )
        stores[-1].start()
    for store in stores:
        store.wait()


def kernel(
    q_hbm,
    k_hbm,
    v_hbm,
    seg_hbm,
    ridge_hbm,
    out_ref,
    late_ref,
    prefix_c,
    q_ref,
    k_ref,
    v_ref,
    seg_ref,
    ridge_ref,
    key_t,
    scales,
    masks,
    query_t,
    first_local,
    send_g,
    recv_g,
    send_c,
    recv_c,
    total_g,
    early_g,
    total_c,
    early_c,
    back_g,
    prefix_g,
    back_c,
    solved,
    load_sem,
    send_sem,
    recv_sem,
    total_send_sem,
    total_recv_sem,
):
    group, me = lax.axis_index("outer"), lax.axis_index("inner")
    me_z, me_x = me // SIDE, lax.rem(me, SIDE)
    peers = [
        lax.rem(me_z + z, SIDE) * SIDE + lax.rem(me_x + x, SIDE) for x, z in OFFSETS
    ]

    def group_at(step):
        return lax.rem(group + OUTER + step, OUTER)

    loads = [
        pltpu.make_async_copy(source, target, load_sem.at[place])
        for place, (source, target) in enumerate(
            (
                (seg_hbm, seg_ref),
                (k_hbm, k_ref),
                (v_hbm, v_ref),
                (q_hbm, q_ref),
                (ridge_hbm, ridge_ref),
            )
        )
    ]
    for load in loads:
        load.start()

    barrier = pltpu.get_barrier_semaphore()
    for peer in peers:
        pl.semaphore_signal(barrier, inc=1, device_id=(group, peer), device_id_type=MESH)
    for step in (-2, -1, 1, 2):
        pl.semaphore_signal(barrier, inc=1, device_id=(group_at(step), me), device_id_type=MESH)

    def send(kind, source, target, rows, peer):
        return pltpu.make_async_remote_copy(
            src_ref=source.at[peer, rows],
            dst_ref=target.at[me, rows],
            send_sem=send_sem.at[kind],
            recv_sem=recv_sem.at[kind],
            device_id=(group, peer),
            device_id_type=MESH,
        )

    def start_last(kind, source, target, rows):
        parity = lax.rem(me_z, 2)
        for z in (parity, 1 - parity, 2 + parity, 3 - parity):
            for step in (2, 1, 3):
                peer = z * SIDE + lax.rem(me_x + step, SIDE)
                send(kind, source, target, rows, peer).start()

            @pl.when(z != me_z)
            def _():
                send(kind, source, target, rows, z * SIDE + me_x).start()

        target[me, rows] = source[me, rows]

    def start_all(kind, source, target, rows):
        for peer in peers:
            send(kind, source, target, rows, peer).start()
        target[me, rows] = source[me, rows]

    def all_of(kind, source, target, rows):
        blocks = pl.ds(0, INNER - 1)
        return pltpu.make_async_remote_copy(
            src_ref=source.at[blocks, rows],
            dst_ref=target.at[blocks, rows],
            send_sem=send_sem.at[kind],
            recv_sem=recv_sem.at[kind],
            device_id=(group, peers[0]),
            device_id_type=MESH,
        )

    def pass_on(kind, source, target, step, rows):
        return pltpu.make_async_remote_copy(
            src_ref=source.at[rows],
            dst_ref=target.at[step - 1, rows],
            send_sem=total_send_sem.at[kind, step - 1],
            recv_sem=total_recv_sem.at[kind, step - 1],
            device_id=(group_at(step), me),
            device_id_type=MESH,
        )

    loads[0].wait()
    row = lax.broadcasted_iota(jnp.int32, (ROWS, ROWS), 0)
    col = lax.broadcasted_iota(jnp.int32, (ROWS, ROWS), 1)
    info_row = lax.broadcasted_iota(jnp.int32, (INFO, WIDTH), 0)
    seg_cols = jnp.broadcast_to(seg_ref[...].astype(F32), (ROWS, ROWS))
    seg_rows = seg_cols.T
    first, last = seg_rows[0:1], seg_rows[ROWS - 1 :]
    weight = (seg_cols[0:1] == last).astype(F32)
    same = seg_rows == seg_cols
    within = jnp.logical_and(row >= col, same).astype(F32)
    within_t = jnp.logical_and(col >= row, same).astype(F32)
    carried_t = (seg_cols[0:1] == first).astype(F32)
    ids = jnp.where(info_row == 1, last, jnp.where(info_row == 2, first, 0.0))
    whole, lower, upper = pl.ds(0, PART), pl.ds(0, HALF), pl.ds(HALF, HALF)
    sent = pl.ds(0, HALF + 3)
    returned = pl.ds(0, HALF + 1)

    def head_slice(head):
        return pl.ds(pl.multiple_of(head * WIDTH, WIDTH), WIDTH)

    def gram(head):
        keys = k_ref[:, head_slice(head)]
        turned = keys.astype(F32).T
        scale = lax.rsqrt(jnp.sum(turned * turned, 0, keepdims=True) + 1e-06)
        key_t[head] = turned.astype(BF16)
        scales[head] = jnp.broadcast_to(scale, (INFO, WIDTH))
        return mm_split(turned * (weight * scale * scale), twice(keys))

    def gram_pair(pair, carry):
        one, two = gram(2 * pair), gram(2 * pair + 1)
        joined = jnp.where(row <= col, one, two)
        diagonal = jnp.sum(jnp.where(row == col, two, 0.0), 0, keepdims=True)
        info = jnp.where(info_row == 0, diagonal, ids)
        send_g[2 * pair, 0:HALF] = joined[0:HALF]
        send_g[2 * pair + 1, 0:HALF] = joined[HALF:]
        send_g[2 * pair, HALF:PART] = info
        send_g[2 * pair + 1, HALF:PART] = info
        return carry

    loads[1].wait()
    lax.fori_loop(0, HEADS // 2, gram_pair, 0, unroll=2)
    pl.semaphore_wait(barrier, INNER - 1 + 4)
    start_all(0, send_g, recv_g, sent)

    def cross(head, carry):
        turned = key_t[head].astype(F32) * (weight * scales[head, 0:1])
        send_c[head] = mm_split(turned, twice(v_ref[:, head_slice(head)]))
        return carry

    loads[2].wait()
    lax.fori_loop(0, HEADS, cross, 0, unroll=4)
    start_all(1, send_c, recv_c, lower)
    start_all(2, send_c, recv_c, upper)

    def prepare(head, carry):
        cols = head_slice(head)
        keys = k_ref[:, cols]
        widened = keys.astype(F32)
        scale = lax.rsqrt(jnp.sum(widened * widened, -1, keepdims=True) + 1e-06)
        mask = within_t * (scale * scale)
        masks[head] = mask
        query = q_ref[:, cols].astype(F32).T
        query = query * lax.rsqrt(jnp.sum(query * query, 0, keepdims=True) + 1e-06)
        query_t[head] = query
        scores = mm(twice_wide(keys), jnp.concatenate(halves(query), 0)) * mask
        local = mm(twice_wide(key_t[head]), jnp.concatenate(halves(scores), 0))
        first_local[head] = local + ridge_ref[head] * query
        return carry

    def prepare_some(some):
        lax.fori_loop(4 * some, 4 * some + 4, prepare, 0, unroll=2)

    loads[3].wait()
    loads[4].wait()
    prepare_some(0)

    def last_of(shard):
        return recv_g[shard, HALF + 1 : HALF + 2]

    def first_of(shard):
        return recv_g[shard, HALF + 2 : HALF + 3]

    def total_of(received, rows):
        final = last_of(INNER - 1)
        summed = received[INNER - 1, rows]
        for shard in range(INNER - 1):
            summed = summed + jnp.where(last_of(shard) == final, received[shard, rows], 0.0)
        return summed

    has_one = (jnp.zeros((1, WIDTH), jnp.int32) + group) >= 1
    has_two = (jnp.zeros((1, WIDTH), jnp.int32) + group) >= 2

    def early_last(which):
        return early_g[which, HALF + 1 : HALF + 2]

    def prefixes(received, early, back, rows):
        running_last = jnp.where(has_one, early_last(0), -1.0)
        second = jnp.where(
            jnp.logical_and(has_two, early_last(1) == running_last), early[1, rows], 0.0
        )
        running = jnp.where(has_one, early[0, rows], 0.0) + second
        for shard in range(INNER):
            back[shard, rows] = jnp.where(running_last == first_of(shard), running, 0.0)
            own_last = last_of(shard)
            running = received[shard, rows] + jnp.where(running_last == own_last, running, 0.0)
            running_last = own_last

    def hand_on(kind, source, target, rows):
        for step in (1, 2):
            pass_on(kind, source, target, step, rows).start()

    def take(kind, source, target, rows):
        for step in (1, 2):
            pass_on(kind, source, target, step, rows).wait_recv()

    all_of(0, send_g, recv_g, sent).wait_recv()
    summed = total_of(recv_g, whole)
    total_g[0:HALF] = summed[0:HALF]
    total_g[HALF:PART] = jnp.where(
        info_row == 0, summed[HALF:PART], recv_g[INNER - 1, HALF:PART]
    )
    hand_on(0, total_g, early_g, sent)
    prepare_some(1)
    take(0, total_g, early_g, sent)
    prefixes(recv_g, early_g, back_g, whole)
    start_all(3, back_g, prefix_g, returned)

    for kind, rows in ((1, lower), (2, upper)):
        all_of(kind, send_c, recv_c, rows).wait_recv()
        total_c[rows] = total_of(recv_c, rows)
        hand_on(kind, total_c, early_c, rows)
        prepare_some(kind + 1)
        take(kind, total_c, early_c, rows)
        prefixes(recv_c, early_c, back_c, rows)
        (start_last if kind + 3 == LAST else start_all)(kind + 3, back_c, prefix_c, rows)

    all_of(3, back_g, prefix_g, returned).wait_recv()

    def solve(heads, grams):
        mats, pairs, searches, remains, squares, answers = [], [], [], [], [], []
        for head, gram_in in zip(heads, grams):
            keys = k_ref[:, head_slice(head)]
            mats.append(twice_wide(jnp.concatenate([*halves(gram_in), keys], 0)))
            pairs.append(twice_wide(key_t[head]))
            query = query_t[head]
            searches.append(query)
            remains.append(query)
            squares.append(jnp.sum(query * query, 0, keepdims=True))
            answers.append(None)
        count = range(len(heads))
        for step in range(CG_ITERS):
            stacks = [jnp.concatenate(halves(searches[n]), 0) for n in count]
            if step == 0:
                products = [mm(mats[n][: 2 * WIDTH], stacks[n]) for n in count]
                locals_ = [first_local[heads[n]] for n in count]
            else:
                products = [mm(mats[n], stacks[n]) for n in count]
                scores = [products[n][2 * WIDTH :] * masks[heads[n]] for n in count]
                locals_ = [
                    mm(pairs[n], jnp.concatenate(halves(scores[n]), 0))
                    + ridge_ref[heads[n]] * searches[n]
                    for n in count
                ]
            applied = [
                (products[n][:WIDTH] + products[n][WIDTH : 2 * WIDTH]) * carried_t + locals_[n]
                for n in count
            ]
            sizes = [
                squares[n] / jnp.sum(searches[n] * applied[n], 0, keepdims=True) for n in count
            ]
            for n in count:
                move = sizes[n] * searches[n]
                answers[n] = move if step == 0 else answers[n] + move
            if step < CG_ITERS - 1:
                remains = [remains[n] - sizes[n] * applied[n] for n in count]
                nexts = [jnp.sum(remains[n] * remains[n], 0, keepdims=True) for n in count]
                searches = [
                    remains[n] + (nexts[n] / squares[n]) * searches[n] for n in count
                ]
                squares = nexts
        for n in count:
            head = heads[n]
            solved[head] = answers[n].T

    def solve_some(some, carry):
        heads, grams = [], []
        for offset in range(GROUP // 2):
            pair = some * (GROUP // 2) + offset
            joined = jnp.concatenate(
                [prefix_g[2 * pair, 0:HALF], prefix_g[2 * pair + 1, 0:HALF]], 0
            )
            turned = joined.T
            diagonal = prefix_g[2 * pair, HALF : HALF + 1]
            grams.append(jnp.where(row <= col, joined, turned))
            grams.append(
                jnp.where(row == col, diagonal, jnp.where(row > col, joined, turned))
            )
            heads += [2 * pair, 2 * pair + 1]
        solve(heads, grams)
        return carry

    lax.fori_loop(0, HEADS // GROUP, solve_some, 0)

    def read_out(head, carry):
        cols = head_slice(head)
        scale = scales[head, 0:1]
        scores = mm_split(solved[head], twice(key_t[head])) * (within * scale)
        out_ref[:, cols] = mm_split(scores, twice(v_ref[:, cols]))
        return carry

    lax.fori_loop(0, HEADS, read_out, 0, unroll=8)
    carried = (seg_rows == first).astype(F32)

    def add_lower(head, carry):
        cols = head_slice(head)
        high, low = halves(solved[head] * carried)
        late_ref[head] = jnp.concatenate([high[:, HALF:], low[:, HALF:]], 1)
        out_ref[:, cols] = out_ref[:, cols] + cross_part(
            high[:, :HALF], low[:, :HALF], prefix_c[head, lower]
        )
        return carry

    all_of(0, send_g, recv_g, sent).wait_send()
    for kind, rows in ((1, lower), (2, upper)):
        all_of(kind, send_c, recv_c, rows).wait_send()
    all_of(3, back_g, prefix_g, returned).wait_send()
    for step in (1, 2):
        pass_on(0, total_g, early_g, step, sent).wait_send()
        pass_on(1, total_c, early_c, step, lower).wait_send()
        pass_on(2, total_c, early_c, step, upper).wait_send()
    all_of(4, back_c, prefix_c, lower).wait_recv()
    lax.fori_loop(0, HEADS, add_lower, 0, unroll=8)
    all_of(4, back_c, prefix_c, lower).wait_send()

    all_of(LAST, back_c, prefix_c, upper).wait_recv()
    all_of(LAST, back_c, prefix_c, upper).wait_send()


def on_device(queries, key_vectors, value_vectors, segment_ids, ridge_weight):
    vmem = pl.BlockSpec(memory_space=pltpu.VMEM)
    hbm = pl.BlockSpec(memory_space=pltpu.HBM)
    operand = pltpu.VMEM((ROWS, HEADS * WIDTH), BF16)
    state_g = pltpu.VMEM((INNER, PART, WIDTH), F32)
    state_c = pltpu.VMEM((INNER, ROWS, WIDTH), F32)
    part, late, state = pl.pallas_call(
        kernel,
        name="mesa",
        out_shape=(
            jax.ShapeDtypeStruct((ROWS, HEADS * WIDTH), F32),
            jax.ShapeDtypeStruct((HEADS, ROWS, WIDTH), BF16),
            jax.ShapeDtypeStruct((INNER, ROWS, WIDTH), F32),
        ),
        in_specs=[hbm] * 5,
        out_specs=(vmem, vmem, vmem),
        scratch_shapes=[
            operand,
            operand,
            operand,
            pltpu.VMEM((1, ROWS), jnp.int32),
            pltpu.SMEM((HEADS,), F32),
            pltpu.VMEM((HEADS, WIDTH, ROWS), BF16),
            pltpu.VMEM((HEADS, INFO, WIDTH), F32),
            state_c,
            state_c,
            state_c,
            state_g,
            state_g,
            state_c,
            state_c,
            pltpu.VMEM((PART, WIDTH), F32),
            pltpu.VMEM((2, PART, WIDTH), F32),
            pltpu.VMEM((ROWS, WIDTH), F32),
            pltpu.VMEM((2, ROWS, WIDTH), F32),
            state_g,
            state_g,
            state_c,
            state_c,
            pltpu.SemaphoreType.DMA((5,)),
            pltpu.SemaphoreType.DMA((6,)),
            pltpu.SemaphoreType.DMA((6,)),
            pltpu.SemaphoreType.DMA((3, 2)),
            pltpu.SemaphoreType.DMA((3, 2)),
        ],
        compiler_params=pltpu.CompilerParams(
            collective_id=0, has_side_effects=True, vmem_limit_bytes=48 << 20
        ),
    )(
        *(
            pltpu.with_memory_space_constraint(value, pltpu.HBM)
            for value in (
                queries,
                key_vectors,
                value_vectors,
                segment_ids.reshape(1, ROWS),
                ridge_weight,
            )
        ),
    )
    return pl.pallas_call(
        finish,
        name="finish",
        out_shape=jax.ShapeDtypeStruct((ROWS, HEADS * WIDTH), F32),
        in_specs=[vmem, vmem, vmem],
        out_specs=hbm,
        scratch_shapes=[
            pltpu.VMEM((ROWS, HEADS * WIDTH), F32),
            pltpu.SemaphoreType.DMA((STEPS,)),
        ],
        compiler_params=pltpu.CompilerParams(vmem_limit_bytes=16 << 20),
    )(part, late, state)


def solution(mesh):
    spec = P(("outer", "inner"), None)
    return jax.shard_map(
        on_device,
        mesh=mesh,
        in_specs=(spec, spec, spec, P(("outer", "inner")), P()),
        out_specs=spec,
        check_vma=False,
    )
```

```python
import jax
import jax.numpy as jnp
from jax import lax
from jax.experimental import pallas as pl
from jax.experimental.pallas import tpu as pltpu
from jax.sharding import PartitionSpec as P

CG_ITERS = 3
HEADS = 16
WIDTH = 128
ROWS = 128
HALF = ROWS // 2
INFO = 8
PART = HALF + INFO
INNER = 16
OUTER = 8
SIDE = 4
GROUP = 8
STEPS = 4
LAST = 5
OFFSETS = sorted(
    ((x, z) for z in range(SIDE) for x in range(SIDE) if (x, z) != (0, 0)),
    key=lambda o: -(min(o[0], SIDE - o[0]) + min(o[1], SIDE - o[1])),
)
MESH = pl.DeviceIdType.MESH
F32 = jnp.float32
BF16 = jnp.bfloat16


def halves(value):
    high = value.astype(BF16)
    return high, (value - high.astype(F32)).astype(BF16)


def mm(left, right):
    return jnp.dot(left, right, preferred_element_type=F32)


def mm_split(value, stacked):
    return mm(jnp.concatenate(halves(value), 1), stacked)


def twice(value):
    return jnp.concatenate([value, value], 0)


def twice_wide(value):
    return jnp.concatenate([value, value], 1)


def cross_part(high, low, state):
    state_high, state_low = halves(state)
    return mm(
        jnp.concatenate([high, low, high], 1),
        jnp.concatenate([state_high, state_high, state_low], 0),
    )


def finish(part_ref, late_ref, state_ref, out_hbm, done, sems):
    stores = []
    for step in range(STEPS):
        for head in range(step * HEADS // STEPS, (step + 1) * HEADS // STEPS):
            late = late_ref[head]
            cols = pl.ds(head * WIDTH, WIDTH)
            done[:, cols] = part_ref[:, cols] + cross_part(
                late[:, :HALF], late[:, HALF:], state_ref[head, HALF:]
            )
        cols = pl.ds(step * HEADS // STEPS * WIDTH, HEADS // STEPS * WIDTH)
        stores.append(
            pltpu.make_async_copy(done.at[:, cols], out_hbm.at[:, cols], sems.at[step])
        )
        stores[-1].start()
    for store in stores:
        store.wait()


def kernel(
    q_hbm,
    k_hbm,
    v_hbm,
    seg_hbm,
    ridge_hbm,
    out_ref,
    late_ref,
    prefix_c,
    q_ref,
    k_ref,
    v_ref,
    seg_ref,
    ridge_ref,
    key_t,
    scales,
    masks,
    query_t,
    first_local,
    send_g,
    recv_g,
    send_c,
    recv_c,
    total_g,
    early_g,
    total_c,
    early_c,
    back_g,
    prefix_g,
    back_c,
    solved,
    load_sem,
    send_sem,
    recv_sem,
    total_send_sem,
    total_recv_sem,
):
    group, me = lax.axis_index("outer"), lax.axis_index("inner")
    me_z, me_x = me // SIDE, lax.rem(me, SIDE)
    peers = [
        lax.rem(me_z + z, SIDE) * SIDE + lax.rem(me_x + x, SIDE) for x, z in OFFSETS
    ]

    def group_at(step):
        return lax.rem(group + OUTER + step, OUTER)

    loads = [
        pltpu.make_async_copy(source, target, load_sem.at[place])
        for place, (source, target) in enumerate(
            (
                (seg_hbm, seg_ref),
                (k_hbm, k_ref),
                (v_hbm, v_ref),
                (q_hbm, q_ref),
                (ridge_hbm, ridge_ref),
            )
        )
    ]
    barrier = pltpu.get_barrier_semaphore()
    for peer in peers:
        pl.semaphore_signal(barrier, inc=1, device_id=(group, peer), device_id_type=MESH)
    for step in (-2, -1, 1, 2):
        pl.semaphore_signal(barrier, inc=1, device_id=(group_at(step), me), device_id_type=MESH)
    for load in loads:
        load.start()

    def send(kind, source, target, rows, peer):
        return pltpu.make_async_remote_copy(
            src_ref=source.at[peer, rows],
            dst_ref=target.at[me, rows],
            send_sem=send_sem.at[kind],
            recv_sem=recv_sem.at[kind],
            device_id=(group, peer),
            device_id_type=MESH,
        )

    def start_last(kind, source, target, rows):
        parity = lax.rem(me_z, 2)
        for z in (parity, 1 - parity, 2 + parity, 3 - parity):
            for step in (2, 1, 3):
                peer = z * SIDE + lax.rem(me_x + step, SIDE)
                send(kind, source, target, rows, peer).start()

            @pl.when(z != me_z)
            def _():
                send(kind, source, target, rows, z * SIDE + me_x).start()

        target[me, rows] = source[me, rows]

    def start_all(kind, source, target, rows):
        for peer in peers:
            send(kind, source, target, rows, peer).start()
        target[me, rows] = source[me, rows]

    def all_of(kind, source, target, rows):
        blocks = pl.ds(0, INNER - 1)
        return pltpu.make_async_remote_copy(
            src_ref=source.at[blocks, rows],
            dst_ref=target.at[blocks, rows],
            send_sem=send_sem.at[kind],
            recv_sem=recv_sem.at[kind],
            device_id=(group, peers[0]),
            device_id_type=MESH,
        )

    def pass_on(kind, source, target, step, rows):
        return pltpu.make_async_remote_copy(
            src_ref=source.at[rows],
            dst_ref=target.at[step - 1, rows],
            send_sem=total_send_sem.at[kind, step - 1],
            recv_sem=total_recv_sem.at[kind, step - 1],
            device_id=(group_at(step), me),
            device_id_type=MESH,
        )

    loads[0].wait()
    row = lax.broadcasted_iota(jnp.int32, (ROWS, ROWS), 0)
    col = lax.broadcasted_iota(jnp.int32, (ROWS, ROWS), 1)
    info_row = lax.broadcasted_iota(jnp.int32, (INFO, WIDTH), 0)
    seg_cols = jnp.broadcast_to(seg_ref[...].astype(F32), (ROWS, ROWS))
    seg_rows = seg_cols.T
    first, last = seg_rows[0:1], seg_rows[ROWS - 1 :]
    weight = (seg_cols[0:1] == last).astype(F32)
    same = seg_rows == seg_cols
    within = jnp.logical_and(row >= col, same).astype(F32)
    within_t = jnp.logical_and(col >= row, same).astype(F32)
    carried_t = (seg_cols[0:1] == first).astype(F32)
    ids = jnp.where(info_row == 1, last, jnp.where(info_row == 2, first, 0.0))
    whole, lower, upper = pl.ds(0, PART), pl.ds(0, HALF), pl.ds(HALF, HALF)
    sent = pl.ds(0, HALF + 3)
    returned = pl.ds(0, HALF + 1)

    def head_slice(head):
        return pl.ds(pl.multiple_of(head * WIDTH, WIDTH), WIDTH)

    def gram(head):
        keys = k_ref[:, head_slice(head)]
        turned = keys.astype(F32).T
        scale = lax.rsqrt(jnp.sum(turned * turned, 0, keepdims=True) + 1e-06)
        key_t[head] = turned.astype(BF16)
        scales[head] = jnp.broadcast_to(scale, (INFO, WIDTH))
        return mm_split(turned * (weight * scale * scale), twice(keys))

    def gram_pair(pair, carry):
        one, two = gram(2 * pair), gram(2 * pair + 1)
        joined = jnp.where(row <= col, one, two)
        diagonal = jnp.sum(jnp.where(row == col, two, 0.0), 0, keepdims=True)
        info = jnp.where(info_row == 0, diagonal, ids)
        send_g[2 * pair, 0:HALF] = joined[0:HALF]
        send_g[2 * pair + 1, 0:HALF] = joined[HALF:]
        send_g[2 * pair, HALF:PART] = info
        send_g[2 * pair + 1, HALF:PART] = info
        return carry

    loads[1].wait()
    lax.fori_loop(0, HEADS // 2, gram_pair, 0, unroll=2)
    pl.semaphore_wait(barrier, INNER - 1 + 4)
    start_all(0, send_g, recv_g, sent)

    def cross(head, carry):
        turned = key_t[head].astype(F32) * (weight * scales[head, 0:1])
        send_c[head] = mm_split(turned, twice(v_ref[:, head_slice(head)]))
        return carry

    loads[2].wait()
    lax.fori_loop(0, HEADS, cross, 0, unroll=4)
    start_all(1, send_c, recv_c, lower)
    start_all(2, send_c, recv_c, upper)

    def prepare(head, carry):
        cols = head_slice(head)
        keys = k_ref[:, cols]
        widened = keys.astype(F32)
        scale = lax.rsqrt(jnp.sum(widened * widened, -1, keepdims=True) + 1e-06)
        mask = within_t * (scale * scale)
        masks[head] = mask
        query = q_ref[:, cols].astype(F32).T
        query = query * lax.rsqrt(jnp.sum(query * query, 0, keepdims=True) + 1e-06)
        query_t[head] = query
        scores = mm(twice_wide(keys), jnp.concatenate(halves(query), 0)) * mask
        local = mm(twice_wide(key_t[head]), jnp.concatenate(halves(scores), 0))
        first_local[head] = local + ridge_ref[head] * query
        return carry

    def prepare_some(some):
        lax.fori_loop(4 * some, 4 * some + 4, prepare, 0, unroll=2)

    loads[3].wait()
    loads[4].wait()
    prepare_some(0)

    def last_of(shard):
        return recv_g[shard, HALF + 1 : HALF + 2]

    def first_of(shard):
        return recv_g[shard, HALF + 2 : HALF + 3]

    def total_of(received, rows):
        final = last_of(INNER - 1)
        summed = received[INNER - 1, rows]
        for shard in range(INNER - 1):
            summed = summed + jnp.where(last_of(shard) == final, received[shard, rows], 0.0)
        return summed

    has_one = (jnp.zeros((1, WIDTH), jnp.int32) + group) >= 1
    has_two = (jnp.zeros((1, WIDTH), jnp.int32) + group) >= 2

    def early_last(which):
        return early_g[which, HALF + 1 : HALF + 2]

    def prefixes(received, early, back, rows):
        running_last = jnp.where(has_one, early_last(0), -1.0)
        second = jnp.where(
            jnp.logical_and(has_two, early_last(1) == running_last), early[1, rows], 0.0
        )
        running = jnp.where(has_one, early[0, rows], 0.0) + second
        for shard in range(INNER):
            back[shard, rows] = jnp.where(running_last == first_of(shard), running, 0.0)
            own_last = last_of(shard)
            running = received[shard, rows] + jnp.where(running_last == own_last, running, 0.0)
            running_last = own_last

    def hand_on(kind, source, target, rows):
        for step in (1, 2):
            pass_on(kind, source, target, step, rows).start()

    def take(kind, source, target, rows):
        for step in (1, 2):
            pass_on(kind, source, target, step, rows).wait_recv()

    all_of(0, send_g, recv_g, sent).wait_recv()
    summed = total_of(recv_g, whole)
    total_g[0:HALF] = summed[0:HALF]
    total_g[HALF:PART] = jnp.where(
        info_row == 0, summed[HALF:PART], recv_g[INNER - 1, HALF:PART]
    )
    hand_on(0, total_g, early_g, sent)
    prepare_some(1)
    take(0, total_g, early_g, sent)
    prefixes(recv_g, early_g, back_g, whole)
    start_all(3, back_g, prefix_g, returned)

    for kind, rows in ((1, lower), (2, upper)):
        all_of(kind, send_c, recv_c, rows).wait_recv()
        total_c[rows] = total_of(recv_c, rows)
        hand_on(kind, total_c, early_c, rows)
        prepare_some(kind + 1)
        take(kind, total_c, early_c, rows)
        prefixes(recv_c, early_c, back_c, rows)
        (start_last if kind + 3 == LAST else start_all)(kind + 3, back_c, prefix_c, rows)

    all_of(3, back_g, prefix_g, returned).wait_recv()

    def solve(heads, grams):
        mats, pairs, searches, remains, squares, answers = [], [], [], [], [], []
        for head, gram_in in zip(heads, grams):
            keys = k_ref[:, head_slice(head)]
            mats.append(twice_wide(jnp.concatenate([*halves(gram_in), keys], 0)))
            pairs.append(twice_wide(key_t[head]))
            query = query_t[head]
            searches.append(query)
            remains.append(query)
            squares.append(jnp.sum(query * query, 0, keepdims=True))
            answers.append(None)
        count = range(len(heads))
        for step in range(CG_ITERS):
            stacks = [jnp.concatenate(halves(searches[n]), 0) for n in count]
            if step == 0:
                products = [mm(mats[n][: 2 * WIDTH], stacks[n]) for n in count]
                locals_ = [first_local[heads[n]] for n in count]
            else:
                products = [mm(mats[n], stacks[n]) for n in count]
                scores = [products[n][2 * WIDTH :] * masks[heads[n]] for n in count]
                locals_ = [
                    mm(pairs[n], jnp.concatenate(halves(scores[n]), 0))
                    + ridge_ref[heads[n]] * searches[n]
                    for n in count
                ]
            applied = [
                (products[n][:WIDTH] + products[n][WIDTH : 2 * WIDTH]) * carried_t + locals_[n]
                for n in count
            ]
            sizes = [
                squares[n] / jnp.sum(searches[n] * applied[n], 0, keepdims=True) for n in count
            ]
            for n in count:
                move = sizes[n] * searches[n]
                answers[n] = move if step == 0 else answers[n] + move
            if step < CG_ITERS - 1:
                remains = [remains[n] - sizes[n] * applied[n] for n in count]
                nexts = [jnp.sum(remains[n] * remains[n], 0, keepdims=True) for n in count]
                searches = [
                    remains[n] + (nexts[n] / squares[n]) * searches[n] for n in count
                ]
                squares = nexts
        for n in count:
            head = heads[n]
            solved[head] = answers[n].T

    def solve_some(some, carry):
        heads, grams = [], []
        for offset in range(GROUP // 2):
            pair = some * (GROUP // 2) + offset
            joined = jnp.concatenate(
                [prefix_g[2 * pair, 0:HALF], prefix_g[2 * pair + 1, 0:HALF]], 0
            )
            turned = joined.T
            diagonal = prefix_g[2 * pair, HALF : HALF + 1]
            grams.append(jnp.where(row <= col, joined, turned))
            grams.append(
                jnp.where(row == col, diagonal, jnp.where(row > col, joined, turned))
            )
            heads += [2 * pair, 2 * pair + 1]
        solve(heads, grams)
        return carry

    lax.fori_loop(0, HEADS // GROUP, solve_some, 0)

    def read_out(head, carry):
        cols = head_slice(head)
        scale = scales[head, 0:1]
        scores = mm_split(solved[head], twice(key_t[head])) * (within * scale)
        out_ref[:, cols] = mm_split(scores, twice(v_ref[:, cols]))
        return carry

    lax.fori_loop(0, HEADS, read_out, 0, unroll=8)
    carried = (seg_rows == first).astype(F32)

    def add_lower(head, carry):
        cols = head_slice(head)
        high, low = halves(solved[head] * carried)
        late_ref[head] = jnp.concatenate([high[:, HALF:], low[:, HALF:]], 1)
        out_ref[:, cols] = out_ref[:, cols] + cross_part(
            high[:, :HALF], low[:, :HALF], prefix_c[head, lower]
        )
        return carry

    all_of(0, send_g, recv_g, sent).wait_send()
    for kind, rows in ((1, lower), (2, upper)):
        all_of(kind, send_c, recv_c, rows).wait_send()
    all_of(3, back_g, prefix_g, returned).wait_send()
    for step in (1, 2):
        pass_on(0, total_g, early_g, step, sent).wait_send()
        pass_on(1, total_c, early_c, step, lower).wait_send()
        pass_on(2, total_c, early_c, step, upper).wait_send()
    all_of(4, back_c, prefix_c, lower).wait_recv()
    lax.fori_loop(0, HEADS, add_lower, 0, unroll=8)
    all_of(4, back_c, prefix_c, lower).wait_send()

    all_of(LAST, back_c, prefix_c, upper).wait_recv()
    all_of(LAST, back_c, prefix_c, upper).wait_send()


def on_device(queries, key_vectors, value_vectors, segment_ids, ridge_weight):
    vmem = pl.BlockSpec(memory_space=pltpu.VMEM)
    hbm = pl.BlockSpec(memory_space=pltpu.HBM)
    operand = pltpu.VMEM((ROWS, HEADS * WIDTH), BF16)
    state_g = pltpu.VMEM((INNER, PART, WIDTH), F32)
    state_c = pltpu.VMEM((INNER, ROWS, WIDTH), F32)
    part, late, state = pl.pallas_call(
        kernel,
        name="mesa",
        out_shape=(
            jax.ShapeDtypeStruct((ROWS, HEADS * WIDTH), F32),
            jax.ShapeDtypeStruct((HEADS, ROWS, WIDTH), BF16),
            jax.ShapeDtypeStruct((INNER, ROWS, WIDTH), F32),
        ),
        in_specs=[hbm] * 5,
        out_specs=(vmem, vmem, vmem),
        scratch_shapes=[
            operand,
            operand,
            operand,
            pltpu.VMEM((1, ROWS), jnp.int32),
            pltpu.SMEM((HEADS,), F32),
            pltpu.VMEM((HEADS, WIDTH, ROWS), BF16),
            pltpu.VMEM((HEADS, INFO, WIDTH), F32),
            state_c,
            state_c,
            state_c,
            state_g,
            state_g,
            state_c,
            state_c,
            pltpu.VMEM((PART, WIDTH), F32),
            pltpu.VMEM((2, PART, WIDTH), F32),
            pltpu.VMEM((ROWS, WIDTH), F32),
            pltpu.VMEM((2, ROWS, WIDTH), F32),
            state_g,
            state_g,
            state_c,
            state_c,
            pltpu.SemaphoreType.DMA((5,)),
            pltpu.SemaphoreType.DMA((6,)),
            pltpu.SemaphoreType.DMA((6,)),
            pltpu.SemaphoreType.DMA((3, 2)),
            pltpu.SemaphoreType.DMA((3, 2)),
        ],
        compiler_params=pltpu.CompilerParams(
            collective_id=0, has_side_effects=True, vmem_limit_bytes=48 << 20
        ),
    )(
        *(
            pltpu.with_memory_space_constraint(value, pltpu.HBM)
            for value in (
                queries,
                key_vectors,
                value_vectors,
                segment_ids.reshape(1, ROWS),
                ridge_weight,
            )
        ),
    )
    return pl.pallas_call(
        finish,
        name="finish",
        out_shape=jax.ShapeDtypeStruct((ROWS, HEADS * WIDTH), F32),
        in_specs=[vmem, vmem, vmem],
        out_specs=hbm,
        scratch_shapes=[
            pltpu.VMEM((ROWS, HEADS * WIDTH), F32),
            pltpu.SemaphoreType.DMA((STEPS,)),
        ],
        compiler_params=pltpu.CompilerParams(vmem_limit_bytes=16 << 20),
    )(part, late, state)


def solution(mesh):
    spec = P(("outer", "inner"), None)
    return jax.shard_map(
        on_device,
        mesh=mesh,
        in_specs=(spec, spec, spec, P(("outer", "inner")), P()),
        out_specs=spec,
        check_vma=False,
    )
```

```python
import jax
import jax.numpy as jnp
from jax import lax
from jax.experimental import pallas as pl
from jax.experimental.pallas import tpu as pltpu
from jax.sharding import PartitionSpec as P

CG_ITERS = 3
HEADS = 16
WIDTH = 128
ROWS = 128
HALF = ROWS // 2
INFO = 8
PART = HALF + INFO
INNER = 16
OUTER = 8
SIDE = 4
GROUP = 8
STEPS = 4
LAST = 5
OFFSETS = sorted(
    ((x, z) for z in range(SIDE) for x in range(SIDE) if (x, z) != (0, 0)),
    key=lambda o: -(min(o[0], SIDE - o[0]) + min(o[1], SIDE - o[1])),
)
MESH = pl.DeviceIdType.MESH
F32 = jnp.float32
BF16 = jnp.bfloat16


def halves(value):
    high = value.astype(BF16)
    return high, (value - high.astype(F32)).astype(BF16)


def mm(left, right):
    return jnp.dot(left, right, preferred_element_type=F32)


def mm_split(value, stacked):
    return mm(jnp.concatenate(halves(value), 1), stacked)


def twice(value):
    return jnp.concatenate([value, value], 0)


def twice_wide(value):
    return jnp.concatenate([value, value], 1)


def cross_part(high, low, state):
    state_high, state_low = halves(state)
    return mm(
        jnp.concatenate([high, low, high], 1),
        jnp.concatenate([state_high, state_high, state_low], 0),
    )


def finish(part_ref, late_ref, state_ref, out_hbm, done, sems):
    stores = []
    for step in range(STEPS):
        for head in range(step * HEADS // STEPS, (step + 1) * HEADS // STEPS):
            late = late_ref[head]
            cols = pl.ds(head * WIDTH, WIDTH)
            done[:, cols] = part_ref[:, cols] + cross_part(
                late[:, :HALF], late[:, HALF:], state_ref[head, HALF:]
            )
        cols = pl.ds(step * HEADS // STEPS * WIDTH, HEADS // STEPS * WIDTH)
        stores.append(
            pltpu.make_async_copy(done.at[:, cols], out_hbm.at[:, cols], sems.at[step])
        )
        stores[-1].start()
    for store in stores:
        store.wait()


def kernel(
    q_hbm,
    k_hbm,
    v_hbm,
    seg_hbm,
    ridge_hbm,
    out_ref,
    late_ref,
    prefix_c,
    q_ref,
    k_ref,
    v_ref,
    seg_ref,
    ridge_ref,
    key_t,
    scales,
    masks,
    query_t,
    first_local,
    send_g,
    recv_g,
    send_c,
    recv_c,
    total_g,
    early_g,
    total_c,
    early_c,
    back_g,
    prefix_g,
    back_c,
    solved,
    load_sem,
    send_sem,
    recv_sem,
    total_send_sem,
    total_recv_sem,
):
    group, me = lax.axis_index("outer"), lax.axis_index("inner")
    me_z, me_x = me // SIDE, lax.rem(me, SIDE)
    peers = [
        lax.rem(me_z + z, SIDE) * SIDE + lax.rem(me_x + x, SIDE) for x, z in OFFSETS
    ]

    def group_at(step):
        return lax.rem(group + OUTER + step, OUTER)

    loads = [
        pltpu.make_async_copy(source, target, load_sem.at[place])
        for place, (source, target) in enumerate(
            (
                (seg_hbm, seg_ref),
                (k_hbm, k_ref),
                (v_hbm, v_ref),
                (q_hbm, q_ref),
                (ridge_hbm, ridge_ref),
            )
        )
    ]
    barrier = pltpu.get_barrier_semaphore()
    for peer in peers:
        pl.semaphore_signal(barrier, inc=1, device_id=(group, peer), device_id_type=MESH)
    for step in (-2, -1, 1, 2):
        pl.semaphore_signal(barrier, inc=1, device_id=(group_at(step), me), device_id_type=MESH)
    for load in loads:
        load.start()

    def send(kind, source, target, rows, peer):
        return pltpu.make_async_remote_copy(
            src_ref=source.at[peer, rows],
            dst_ref=target.at[me, rows],
            send_sem=send_sem.at[kind],
            recv_sem=recv_sem.at[kind],
            device_id=(group, peer),
            device_id_type=MESH,
        )

    def start_last(kind, source, target, rows):
        parity = lax.rem(me_z, 2)
        for turn, z in enumerate((parity, 1 - parity, 3 - parity, 2 + parity)):
            for step in (2, 1, 3) if turn % 2 == 0 else (2, 3, 1):
                peer = z * SIDE + lax.rem(me_x + step, SIDE)
                send(kind, source, target, rows, peer).start()

            @pl.when(z != me_z)
            def _():
                send(kind, source, target, rows, z * SIDE + me_x).start()

        target[me, rows] = source[me, rows]

    def start_all(kind, source, target, rows):
        for peer in peers:
            send(kind, source, target, rows, peer).start()
        target[me, rows] = source[me, rows]

    def all_of(kind, source, target, rows):
        blocks = pl.ds(0, INNER - 1)
        return pltpu.make_async_remote_copy(
            src_ref=source.at[blocks, rows],
            dst_ref=target.at[blocks, rows],
            send_sem=send_sem.at[kind],
            recv_sem=recv_sem.at[kind],
            device_id=(group, peers[0]),
            device_id_type=MESH,
        )

    def pass_on(kind, source, target, step, rows):
        return pltpu.make_async_remote_copy(
            src_ref=source.at[rows],
            dst_ref=target.at[step - 1, rows],
            send_sem=total_send_sem.at[kind, step - 1],
            recv_sem=total_recv_sem.at[kind, step - 1],
            device_id=(group_at(step), me),
            device_id_type=MESH,
        )

    loads[0].wait()
    row = lax.broadcasted_iota(jnp.int32, (ROWS, ROWS), 0)
    col = lax.broadcasted_iota(jnp.int32, (ROWS, ROWS), 1)
    info_row = lax.broadcasted_iota(jnp.int32, (INFO, WIDTH), 0)
    seg_cols = jnp.broadcast_to(seg_ref[...].astype(F32), (ROWS, ROWS))
    seg_rows = seg_cols.T
    first, last = seg_rows[0:1], seg_rows[ROWS - 1 :]
    weight = (seg_cols[0:1] == last).astype(F32)
    same = seg_rows == seg_cols
    within = jnp.logical_and(row >= col, same).astype(F32)
    within_t = jnp.logical_and(col >= row, same).astype(F32)
    carried_t = (seg_cols[0:1] == first).astype(F32)
    ids = jnp.where(info_row == 1, last, jnp.where(info_row == 2, first, 0.0))
    whole, lower, upper = pl.ds(0, PART), pl.ds(0, HALF), pl.ds(HALF, HALF)
    sent = pl.ds(0, HALF + 3)
    returned = pl.ds(0, HALF + 1)

    def head_slice(head):
        return pl.ds(pl.multiple_of(head * WIDTH, WIDTH), WIDTH)

    def gram(head):
        keys = k_ref[:, head_slice(head)]
        turned = keys.astype(F32).T
        scale = lax.rsqrt(jnp.sum(turned * turned, 0, keepdims=True) + 1e-06)
        key_t[head] = turned.astype(BF16)
        scales[head] = jnp.broadcast_to(scale, (INFO, WIDTH))
        return mm_split(turned * (weight * scale * scale), twice(keys))

    def gram_pair(pair, carry):
        one, two = gram(2 * pair), gram(2 * pair + 1)
        joined = jnp.where(row <= col, one, two)
        diagonal = jnp.sum(jnp.where(row == col, two, 0.0), 0, keepdims=True)
        info = jnp.where(info_row == 0, diagonal, ids)
        send_g[2 * pair, 0:HALF] = joined[0:HALF]
        send_g[2 * pair + 1, 0:HALF] = joined[HALF:]
        send_g[2 * pair, HALF:PART] = info
        send_g[2 * pair + 1, HALF:PART] = info
        return carry

    loads[1].wait()
    lax.fori_loop(0, HEADS // 2, gram_pair, 0, unroll=2)
    pl.semaphore_wait(barrier, INNER - 1 + 4)
    start_all(0, send_g, recv_g, sent)

    def cross(head, carry):
        turned = key_t[head].astype(F32) * (weight * scales[head, 0:1])
        send_c[head] = mm_split(turned, twice(v_ref[:, head_slice(head)]))
        return carry

    loads[2].wait()
    lax.fori_loop(0, HEADS, cross, 0, unroll=4)
    start_all(1, send_c, recv_c, lower)
    start_all(2, send_c, recv_c, upper)

    def prepare(head, carry):
        cols = head_slice(head)
        keys = k_ref[:, cols]
        widened = keys.astype(F32)
        scale = lax.rsqrt(jnp.sum(widened * widened, -1, keepdims=True) + 1e-06)
        mask = within_t * (scale * scale)
        masks[head] = mask
        query = q_ref[:, cols].astype(F32).T
        query = query * lax.rsqrt(jnp.sum(query * query, 0, keepdims=True) + 1e-06)
        query_t[head] = query
        scores = mm(twice_wide(keys), jnp.concatenate(halves(query), 0)) * mask
        local = mm(twice_wide(key_t[head]), jnp.concatenate(halves(scores), 0))
        first_local[head] = local + ridge_ref[head] * query
        return carry

    def prepare_some(some):
        lax.fori_loop(4 * some, 4 * some + 4, prepare, 0, unroll=2)

    loads[3].wait()
    loads[4].wait()
    prepare_some(0)

    def last_of(shard):
        return recv_g[shard, HALF + 1 : HALF + 2]

    def first_of(shard):
        return recv_g[shard, HALF + 2 : HALF + 3]

    def total_of(received, rows):
        final = last_of(INNER - 1)
        summed = received[INNER - 1, rows]
        for shard in range(INNER - 1):
            summed = summed + jnp.where(last_of(shard) == final, received[shard, rows], 0.0)
        return summed

    has_one = (jnp.zeros((1, WIDTH), jnp.int32) + group) >= 1
    has_two = (jnp.zeros((1, WIDTH), jnp.int32) + group) >= 2

    def early_last(which):
        return early_g[which, HALF + 1 : HALF + 2]

    def prefixes(received, early, back, rows):
        running_last = jnp.where(has_one, early_last(0), -1.0)
        second = jnp.where(
            jnp.logical_and(has_two, early_last(1) == running_last), early[1, rows], 0.0
        )
        running = jnp.where(has_one, early[0, rows], 0.0) + second
        for shard in range(INNER):
            back[shard, rows] = jnp.where(running_last == first_of(shard), running, 0.0)
            own_last = last_of(shard)
            running = received[shard, rows] + jnp.where(running_last == own_last, running, 0.0)
            running_last = own_last

    def hand_on(kind, source, target, rows):
        for step in (1, 2):
            pass_on(kind, source, target, step, rows).start()

    def take(kind, source, target, rows):
        for step in (1, 2):
            pass_on(kind, source, target, step, rows).wait_recv()

    all_of(0, send_g, recv_g, sent).wait_recv()
    summed = total_of(recv_g, whole)
    total_g[0:HALF] = summed[0:HALF]
    total_g[HALF:PART] = jnp.where(
        info_row == 0, summed[HALF:PART], recv_g[INNER - 1, HALF:PART]
    )
    hand_on(0, total_g, early_g, sent)
    prepare_some(1)
    take(0, total_g, early_g, sent)
    prefixes(recv_g, early_g, back_g, whole)
    start_all(3, back_g, prefix_g, returned)

    for kind, rows in ((1, lower), (2, upper)):
        all_of(kind, send_c, recv_c, rows).wait_recv()
        total_c[rows] = total_of(recv_c, rows)
        hand_on(kind, total_c, early_c, rows)
        prepare_some(kind + 1)
        take(kind, total_c, early_c, rows)
        prefixes(recv_c, early_c, back_c, rows)
        (start_last if kind + 3 == LAST else start_all)(kind + 3, back_c, prefix_c, rows)

    all_of(3, back_g, prefix_g, returned).wait_recv()

    def solve(heads, grams):
        mats, pairs, searches, remains, squares, answers = [], [], [], [], [], []
        for head, gram_in in zip(heads, grams):
            keys = k_ref[:, head_slice(head)]
            mats.append(twice_wide(jnp.concatenate([*halves(gram_in), keys], 0)))
            pairs.append(twice_wide(key_t[head]))
            query = query_t[head]
            searches.append(query)
            remains.append(query)
            squares.append(jnp.sum(query * query, 0, keepdims=True))
            answers.append(None)
        count = range(len(heads))
        for step in range(CG_ITERS):
            stacks = [jnp.concatenate(halves(searches[n]), 0) for n in count]
            if step == 0:
                products = [mm(mats[n][: 2 * WIDTH], stacks[n]) for n in count]
                locals_ = [first_local[heads[n]] for n in count]
            else:
                products = [mm(mats[n], stacks[n]) for n in count]
                scores = [products[n][2 * WIDTH :] * masks[heads[n]] for n in count]
                locals_ = [
                    mm(pairs[n], jnp.concatenate(halves(scores[n]), 0))
                    + ridge_ref[heads[n]] * searches[n]
                    for n in count
                ]
            applied = [
                (products[n][:WIDTH] + products[n][WIDTH : 2 * WIDTH]) * carried_t + locals_[n]
                for n in count
            ]
            sizes = [
                squares[n] / jnp.sum(searches[n] * applied[n], 0, keepdims=True) for n in count
            ]
            for n in count:
                move = sizes[n] * searches[n]
                answers[n] = move if step == 0 else answers[n] + move
            if step < CG_ITERS - 1:
                remains = [remains[n] - sizes[n] * applied[n] for n in count]
                nexts = [jnp.sum(remains[n] * remains[n], 0, keepdims=True) for n in count]
                searches = [
                    remains[n] + (nexts[n] / squares[n]) * searches[n] for n in count
                ]
                squares = nexts
        for n in count:
            head = heads[n]
            solved[head] = answers[n].T

    def solve_some(some, carry):
        heads, grams = [], []
        for offset in range(GROUP // 2):
            pair = some * (GROUP // 2) + offset
            joined = jnp.concatenate(
                [prefix_g[2 * pair, 0:HALF], prefix_g[2 * pair + 1, 0:HALF]], 0
            )
            turned = joined.T
            diagonal = prefix_g[2 * pair, HALF : HALF + 1]
            grams.append(jnp.where(row <= col, joined, turned))
            grams.append(
                jnp.where(row == col, diagonal, jnp.where(row > col, joined, turned))
            )
            heads += [2 * pair, 2 * pair + 1]
        solve(heads, grams)
        return carry

    lax.fori_loop(0, HEADS // GROUP, solve_some, 0)

    def read_out(head, carry):
        cols = head_slice(head)
        scale = scales[head, 0:1]
        scores = mm_split(solved[head], twice(key_t[head])) * (within * scale)
        out_ref[:, cols] = mm_split(scores, twice(v_ref[:, cols]))
        return carry

    lax.fori_loop(0, HEADS, read_out, 0, unroll=8)
    carried = (seg_rows == first).astype(F32)

    def add_lower(head, carry):
        cols = head_slice(head)
        high, low = halves(solved[head] * carried)
        late_ref[head] = jnp.concatenate([high[:, HALF:], low[:, HALF:]], 1)
        out_ref[:, cols] = out_ref[:, cols] + cross_part(
            high[:, :HALF], low[:, :HALF], prefix_c[head, lower]
        )
        return carry

    all_of(0, send_g, recv_g, sent).wait_send()
    for kind, rows in ((1, lower), (2, upper)):
        all_of(kind, send_c, recv_c, rows).wait_send()
    all_of(3, back_g, prefix_g, returned).wait_send()
    for step in (1, 2):
        pass_on(0, total_g, early_g, step, sent).wait_send()
        pass_on(1, total_c, early_c, step, lower).wait_send()
        pass_on(2, total_c, early_c, step, upper).wait_send()
    all_of(4, back_c, prefix_c, lower).wait_recv()
    lax.fori_loop(0, HEADS, add_lower, 0, unroll=8)
    all_of(4, back_c, prefix_c, lower).wait_send()

    all_of(LAST, back_c, prefix_c, upper).wait_recv()
    all_of(LAST, back_c, prefix_c, upper).wait_send()


def on_device(queries, key_vectors, value_vectors, segment_ids, ridge_weight):
    vmem = pl.BlockSpec(memory_space=pltpu.VMEM)
    hbm = pl.BlockSpec(memory_space=pltpu.HBM)
    operand = pltpu.VMEM((ROWS, HEADS * WIDTH), BF16)
    state_g = pltpu.VMEM((INNER, PART, WIDTH), F32)
    state_c = pltpu.VMEM((INNER, ROWS, WIDTH), F32)
    part, late, state = pl.pallas_call(
        kernel,
        name="mesa",
        out_shape=(
            jax.ShapeDtypeStruct((ROWS, HEADS * WIDTH), F32),
            jax.ShapeDtypeStruct((HEADS, ROWS, WIDTH), BF16),
            jax.ShapeDtypeStruct((INNER, ROWS, WIDTH), F32),
        ),
        in_specs=[hbm] * 5,
        out_specs=(vmem, vmem, vmem),
        scratch_shapes=[
            operand,
            operand,
            operand,
            pltpu.VMEM((1, ROWS), jnp.int32),
            pltpu.SMEM((HEADS,), F32),
            pltpu.VMEM((HEADS, WIDTH, ROWS), BF16),
            pltpu.VMEM((HEADS, INFO, WIDTH), F32),
            state_c,
            state_c,
            state_c,
            state_g,
            state_g,
            state_c,
            state_c,
            pltpu.VMEM((PART, WIDTH), F32),
            pltpu.VMEM((2, PART, WIDTH), F32),
            pltpu.VMEM((ROWS, WIDTH), F32),
            pltpu.VMEM((2, ROWS, WIDTH), F32),
            state_g,
            state_g,
            state_c,
            state_c,
            pltpu.SemaphoreType.DMA((5,)),
            pltpu.SemaphoreType.DMA((6,)),
            pltpu.SemaphoreType.DMA((6,)),
            pltpu.SemaphoreType.DMA((3, 2)),
            pltpu.SemaphoreType.DMA((3, 2)),
        ],
        compiler_params=pltpu.CompilerParams(
            collective_id=0, has_side_effects=True, vmem_limit_bytes=48 << 20
        ),
    )(
        *(
            pltpu.with_memory_space_constraint(value, pltpu.HBM)
            for value in (
                queries,
                key_vectors,
                value_vectors,
                segment_ids.reshape(1, ROWS),
                ridge_weight,
            )
        ),
    )
    return pl.pallas_call(
        finish,
        name="finish",
        out_shape=jax.ShapeDtypeStruct((ROWS, HEADS * WIDTH), F32),
        in_specs=[vmem, vmem, vmem],
        out_specs=hbm,
        scratch_shapes=[
            pltpu.VMEM((ROWS, HEADS * WIDTH), F32),
            pltpu.SemaphoreType.DMA((STEPS,)),
        ],
        compiler_params=pltpu.CompilerParams(vmem_limit_bytes=16 << 20),
    )(part, late, state)


def solution(mesh):
    spec = P(("outer", "inner"), None)
    return jax.shard_map(
        on_device,
        mesh=mesh,
        in_specs=(spec, spec, spec, P(("outer", "inner")), P()),
        out_specs=spec,
        check_vma=False,
    )
```
